128 devices in a mesh: grp: 16 (over z, x), nar: 8 (over y, core).
Axes of the slice: x: 4, y: 4, z: 4, core: 2. Of those that a mesh axis runs over, the one named last changes fastest.
Arguments:
- run_desc: bfloat16 [524288, 256], P(('grp', 'nar')), may hold values from -48 to 48
- ref_desc: bfloat16 [8192, 256], P('nar'), may hold values from -6 to 6
- candidates: int32 [4096, 8], P(('grp', 'nar')), may hold values from 0 to 63, as said below
- live_slots: int32 [4096], P(('grp', 'nar')), may hold values from 1 to 8, as said below
- run_mass: float32 [524288], P(('grp', 'nar')), may hold values from 0.1 to 2
- ref_mass: float32 [8192], P('nar'), may hold values from 0.1 to 2
- ref_start: float32 [8192], P('nar'), may hold values from -62 to 42
Outputs:
- run_potential: float32 [524288], P(('grp', 'nar'))
- ref_potential: float32 [8192], P('nar')
The draws below stay inside these ranges and needn't reach their ends.
Inputs may be any that keep to these rules, and one draw needn't show every extreme that they name: `candidates`: each row holds 8 different reference block numbers; every reference block is the first entry of some row. `live_slots`: the first run block of each device has all 8 slots live.
All inputs are finite; a program needn't handle non-finite values.
Results may differ from the reference program's by a relative error of at most 0.0003.
Values may be sent and summed in bfloat16 or wider, within the bound.
A program may use at most 128 MiB of HBM per device.

```python
import math
import jax
import jax.numpy as jnp
from jax import lax

D = 256
BLK = 128
TOPC = 8
ITERS = 3
RB_DEV = 32
RUNB = 4096
ROWS = 524288
REFB = 64
REF = 8192


def block_order(key):
    return jax.random.permutation(jax.random.fold_in(key, 301), REFB).astype(jnp.int32)


def candidate_table(key):
    key_scores = jax.random.fold_in(key, 302)
    run_index = jnp.arange(RUNB, dtype=jnp.int32)
    shuffled = block_order(key)
    leading = shuffled[run_index % REFB]
    rank_keys = jax.random.randint(key_scores, (RUNB, REFB - 1), 0, 1 << 20, dtype=jnp.int32)
    rank_keys = rank_keys * REFB + jnp.arange(REFB - 1, dtype=jnp.int32)[None, :]
    ordering = jnp.argsort(rank_keys, axis=1, stable=True).astype(jnp.int32)
    offsets = 1 + ordering[:, :TOPC - 1]
    trailing = (leading[:, None] + offsets) % REFB
    return jnp.concatenate([leading[:, None], trailing], axis=1).astype(jnp.int32)


def reference_base(key):
    drawn = jax.random.normal(jax.random.fold_in(key, 321), (REF, D), jnp.float32)
    drawn = jnp.clip(drawn, -6.0, 6.0)
    return drawn


def draw_candidates(key, part):
    return candidate_table(key)


def draw_live_slots(key, part):
    key_counts = jax.random.fold_in(key, 311)
    key_caps = jax.random.fold_in(key, 312)
    run_index = jnp.arange(RUNB, dtype=jnp.int32)
    drawn = jax.random.randint(key_counts, (RUNB,), 1, TOPC + 1, dtype=jnp.int32)
    device_cap = jax.random.randint(key_caps, (RUNB // RB_DEV,), 1, TOPC + 1, dtype=jnp.int32)
    capped = jnp.minimum(drawn, device_cap[run_index // RB_DEV])
    capped = jnp.where(run_index % RB_DEV == 0, TOPC, capped)
    capped = jnp.where(run_index == RB_DEV - 1, 1, capped)
    return capped.astype(jnp.int32)


def draw_ref_desc(key, part):
    return reference_base(key).astype(jnp.bfloat16)


def draw_run_desc(key, part):
    drawn = jax.random.normal(jax.random.fold_in(key, 331), (ROWS, D), jnp.float32)
    drawn = jnp.clip(drawn, -6.0, 6.0)
    ref_rows = reference_base(key)
    leading = candidate_table(key)[:, 0]
    chosen_blocks = (RUNB + 15) // 16
    picks = jnp.arange(3 * chosen_blocks, dtype=jnp.int32)
    run_rows = picks // 3 * 16 * BLK + picks % 3
    target = ref_rows[leading[picks // 3 * 16] * BLK]
    widen = 16.0 / math.sqrt(D)
    strength = widen * jnp.where(picks % 3 == 0, 3.2, 6.4)[:, None]
    extra = jnp.where(picks % 3 == 2, 0.6, 0.0)[:, None] * drawn[run_rows]
    drawn = drawn.at[run_rows].set(jnp.clip(strength * target + extra, -48.0, 48.0))
    return drawn.astype(jnp.bfloat16)


def draw_ref_start(key, part):
    cold_count = max(1, REFB // 16)
    shuffled = block_order(key)
    cold_block = jnp.zeros((REFB,), jnp.int32).at[shuffled[:cold_count]].set(1)
    hot_column = jax.random.randint(jax.random.fold_in(key, 344), (REFB,), 2, BLK, dtype=jnp.int32)
    cold_pick = jax.random.randint(jax.random.fold_in(key, 345), (REF,), 0, 8, dtype=jnp.int32)
    feature = jnp.arange(REF, dtype=jnp.int32)
    column = feature % BLK
    block = feature // BLK
    is_hot = column == hot_column[block]
    in_cold_block = cold_block[block] == 1
    cold_jitter = jnp.clip(jax.random.normal(jax.random.fold_in(key, 342), (REF,), jnp.float32), -3.0, 3.0)
    hot_jitter = jnp.clip(jax.random.normal(jax.random.fold_in(key, 346), (REF,), jnp.float32), -3.0, 3.0)
    drawn = jnp.clip(jax.random.normal(jax.random.fold_in(key, 341), (REF,), jnp.float32), -4.0, 4.0)
    is_cold = (cold_pick == 0) & jnp.logical_not(is_hot)
    cold_value = -60.0 + 0.5 * cold_jitter
    drawn = jnp.where(is_cold, cold_value, drawn)
    drawn = jnp.where(is_hot, 40.0 + 0.5 * hot_jitter, drawn)
    drawn = jnp.where(in_cold_block, cold_value, drawn)
    return drawn


def level_of(key, shape, cuts, least, high):
    loudness = 1.0
    for dim, blocks in cuts:
        draws = jax.random.uniform(jax.random.fold_in(jax.random.fold_in(key, 6), dim), (blocks,), jnp.float32, least / len(cuts), high / len(cuts))
        loudness = loudness * jnp.repeat(jnp.exp(draws), shape[dim] // blocks).reshape((-1,) + (1,) * (len(shape) - 1 - dim))
    return loudness


def setup_inputs(seed: int = 0) -> dict:
    seeds = jax.random.split(jax.random.key(seed), 8)
    return {
        "run_desc": draw_run_desc(jax.random.fold_in(seeds[7], 71), 0),
        "ref_desc": draw_ref_desc(jax.random.fold_in(seeds[7], 71), 0),
        "candidates": draw_candidates(jax.random.fold_in(seeds[7], 71), 0),
        "live_slots": draw_live_slots(jax.random.fold_in(seeds[7], 71), 0),
        "run_mass": jnp.clip(jnp.exp(math.log(2.0) - 2.9957323 * jax.random.uniform(seeds[4], (ROWS,), jnp.float32) ** level_of(seeds[4], (ROWS,), ((0, 128),), -0.2, 0.2)), 0.1, 2.0),
        "ref_mass": jnp.clip(jnp.exp(math.log(2.0) - 2.9957323 * jax.random.uniform(seeds[5], (REF,), jnp.float32) ** level_of(seeds[5], (REF,), ((0, 8),), -0.2, 0.2)), 0.1, 2.0),
        "ref_start": draw_ref_start(jax.random.fold_in(seeds[7], 71), 0),
    }


entropic = 0.5
floor_value = -1e+30

def tile_costs(run_desc, ref_desc, candidates):
    group_size = math.gcd(RUNB, 32)
    run_tiles = run_desc.reshape(RUNB // group_size, group_size, BLK, D)
    ref_tiles = ref_desc.reshape(REFB, BLK, D)
    picked_ids = candidates.reshape(RUNB // group_size, group_size, TOPC)

    def one_group(pieces):
        run_piece, id_piece = pieces
        picked = ref_tiles[id_piece].astype(jnp.float32)
        products = jnp.einsum('gid,gtjd->gtij', run_piece.astype(jnp.float32), picked)
        return -products / math.sqrt(D)
    tile_cost = lax.map(one_group, (run_tiles, picked_ids))
    return tile_cost.reshape(RUNB // group_size, group_size, TOPC, BLK, BLK)

def run_side(tile_cost, ref_potential, candidates, live_mask, run_mass):
    group_size = tile_cost.shape[1]
    picked = ref_potential.reshape(REFB, BLK)[candidates]
    picked = picked.reshape(RUNB // group_size, group_size, TOPC, BLK)
    masks = live_mask.reshape(RUNB // group_size, group_size, TOPC)

    def one_group(pieces):
        cost_piece, pick_piece, mask_piece = pieces
        scores = (pick_piece[:, :, None, :] - cost_piece) / entropic
        scores = jnp.where(mask_piece[:, :, None, None], scores, floor_value)
        row_peak = lax.optimization_barrier(jnp.max(scores, axis=(1, 3)))
        row_total = lax.optimization_barrier(jnp.sum(jnp.exp(scores - row_peak[:, None, :, None]), axis=(1, 3)))
        return (row_peak, row_total)
    row_peak, row_total = lax.map(one_group, (tile_cost, picked, masks))
    return entropic * jnp.log(run_mass) - entropic * (row_peak.reshape(-1) + jnp.log(row_total.reshape(-1)))

def ref_side(tile_cost, run_potential, candidates, live_mask, ref_mass):
    group_size = tile_cost.shape[1]
    runs_grouped = run_potential.reshape(RUNB // group_size, group_size, BLK)
    masks = live_mask.reshape(RUNB // group_size, group_size, TOPC)
    flat_ids = candidates.reshape(-1)

    def group_scores(cost_piece, run_piece, mask_piece):
        scores = (run_piece[:, None, :, None] - cost_piece) / entropic
        return jnp.where(mask_piece[:, :, None, None], scores, floor_value)

    def peaks_group(pieces):
        cost_piece, run_piece, mask_piece = pieces
        return lax.optimization_barrier(jnp.max(group_scores(cost_piece, run_piece, mask_piece), axis=2))
    col_peaks = lax.map(peaks_group, (tile_cost, runs_grouped, masks)).reshape(RUNB * TOPC, BLK)
    col_peak = jnp.full((REFB, BLK), floor_value, dtype=jnp.float32).at[flat_ids].max(col_peaks)
    peak_picked = col_peak[candidates].reshape(RUNB // group_size, group_size, TOPC, BLK)

    def totals_group(pieces):
        cost_piece, run_piece, mask_piece, peak_piece = pieces
        scores = group_scores(cost_piece, run_piece, mask_piece)
        return lax.optimization_barrier(jnp.sum(jnp.exp(scores - peak_piece[:, :, None, :]), axis=2))
    col_totals = lax.map(totals_group, (tile_cost, runs_grouped, masks, peak_picked)).reshape(RUNB * TOPC, BLK)
    col_total = jnp.zeros((REFB, BLK), dtype=jnp.float32).at[flat_ids].add(col_totals)
    log_mass = jnp.log(ref_mass).reshape(REFB, BLK)
    return (entropic * log_mass - entropic * (col_peak + jnp.log(col_total))).reshape(-1)

def reference(run_desc, ref_desc, candidates, live_slots, run_mass, ref_mass, ref_start):
    tile_cost = tile_costs(run_desc, ref_desc, candidates)
    live_mask = jnp.arange(TOPC, dtype=jnp.int32)[None, :] < live_slots[:, None]
    ref_potential = ref_start
    run_potential = jnp.zeros((ROWS,), dtype=jnp.float32)
    for iteration in range(ITERS):
        run_potential = run_side(tile_cost, ref_potential, candidates, live_mask, run_mass)
        ref_potential = ref_side(tile_cost, run_potential, candidates, live_mask, ref_mass)
    return (run_potential, ref_potential)
```

```python
import math

import jax
import jax.numpy as jnp
from jax import lax
from jax.experimental import pallas as pl
from jax.experimental.pallas import tpu as pltpu
from jax.sharding import PartitionSpec as P

BLK = 128
TOPC = 8
RB = 32
ENT = RB * TOPC
D = 256
REFB = 64
NAR = 8
GRP = 16
LOG2E = math.log2(math.e)
LN2 = math.log(2.0)
FLOOR = -1e30
MESH = pl.DeviceIdType.MESH
F32 = jnp.float32
BF16 = jnp.bfloat16


def kernel(
    cand,
    live,
    run_hbm,
    ref_hbm,
    run_mass,
    ref_mass,
    start,
    out_run,
    out_ref,
    ref_all,
    run_v,
    tiles,
    v_all,
    rows_a,
    rows_m,
    rows_t,
    rows_live,
    onehot_t,
    onehot,
    a_col,
    loga_col,
    r_col,
    u_col,
    dense,
    peak,
    rs_buf,
    part,
    ar_buf,
    final,
    ag_buf,
    local_sem,
    own_send,
    gather_send,
    gather_recv,
    pair_send,
    pair_recv,
    start_send,
    start_recv,
    rs_send,
    rs_recv,
    ar_send,
    ar_recv,
    ag_send,
    ag_recv,
):
    g = lax.axis_index("grp")
    n = lax.axis_index("nar")
    z, x = lax.div(g, 4), lax.rem(g, 4)
    y, c = lax.div(n, 2), lax.rem(n, 2)

    barrier = pltpu.get_barrier_semaphore()
    for k in range(1, NAR):
        pl.semaphore_signal(
            barrier, inc=1, device_id=(g, lax.rem(n + k, NAR)), device_id_type=MESH
        )
    for k in range(1, GRP):
        pl.semaphore_signal(
            barrier, inc=1, device_id=(lax.rem(g + k, GRP), n), device_id_type=MESH
        )

    own_copy = pltpu.make_async_copy(ref_hbm, ref_all.at[pl.ds(n * 8, 8)], local_sem.at[0])
    own_copy.start()
    run_copy = pltpu.make_async_copy(run_hbm, run_v, local_sem.at[1])
    run_copy.start()

    pl.semaphore_wait(barrier, NAR + GRP - 2)

    partner = (g, y * 2 + 1 - c)
    y_next = (g, lax.rem(y + 1, 4) * 2 + c)
    y_prev = (g, lax.rem(y + 3, 4) * 2 + c)
    x_next = (z * 4 + lax.rem(x + 1, 4), n)
    x_prev = (z * 4 + lax.rem(x + 3, 4), n)
    z_next = (lax.rem(z + 1, 4) * 4 + x, n)
    z_prev = (lax.rem(z + 3, 4) * 4 + x, n)
    s_prev = y_prev[1]
    s_next = y_next[1]
    s_far = lax.rem(y + 2, 4) * 2 + c

    sent = []

    def send(src, dst, send_sem, recv_sem, to):
        copy = pltpu.make_async_remote_copy(
            src_ref=src,
            dst_ref=dst,
            send_sem=send_sem,
            recv_sem=recv_sem,
            device_id=to,
            device_id_type=MESH,
        )
        copy.start()
        sent.append(copy)

    def arrived(dst, recv_sem):
        pltpu.make_async_remote_copy(
            src_ref=dst,
            dst_ref=dst,
            send_sem=own_send.at[0],
            recv_sem=recv_sem,
            device_id=partner,
            device_id_type=MESH,
        ).wait_recv()

    counter = [0]

    def region(block, half):
        if half is None:
            return ref_all.at[block]
        return ref_all.at[block, pl.ds(half * 64, 64)]

    def gsend(block, half, ident, to, src=None):
        dst = region(block, half)
        k = counter[0]
        counter[0] += 1
        send(dst if src is None else src, dst, gather_send.at[k], gather_recv.at[ident], to)

    def to_partner(block, half, ident):
        dst = region(block, half)
        send(dst, dst, pair_send.at[ident], pair_recv.at[ident], partner)

    own_a, own_b = n * 8 + x, n * 8 + 4 + z
    gsend(own_a, None, 0, y_next, ref_hbm.at[x])
    gsend(own_a, None, 1, y_prev, ref_hbm.at[x])
    gsend(own_b, None, 2, y_next, ref_hbm.at[4 + z])
    gsend(own_b, None, 3, y_prev, ref_hbm.at[4 + z])
    for k in range(1, NAR):
        send(
            start,
            v_all.at[pl.ds(n * 8, 8)],
            start_send.at[k],
            start_recv.at[k],
            (g, lax.rem(n + k, NAR)),
        )
    send(ref_hbm, ref_all.at[pl.ds(n * 8, 8)], pair_send.at[30], pair_recv.at[30], partner)
    v_all[pl.ds(n * 8, 8)] = start[...]

    lane64 = lax.broadcasted_iota(jnp.int32, (1, BLK), 1)

    def table_step(b, carry):
        for t in range(TOPC):
            e = b * TOPC + t
            onehot_t[pl.ds(e, 1)] = jnp.where(lane64 == cand[b, t], 1.0, 0.0).astype(F32)
            rows_live[pl.ds(e, 1)] = jnp.where(
                jnp.full((1, BLK), t, jnp.int32) < live[b], 1.0, 0.0
            ).astype(F32)
        return carry

    lax.fori_loop(0, RB, table_step, 0)

    a_prev, a_next, a_far = s_prev * 8 + x, s_next * 8 + x, s_far * 8 + x
    b_prev, b_next, b_far = s_prev * 8 + 4 + z, s_next * 8 + 4 + z, s_far * 8 + 4 + z

    def y_piece(block, ident, j, along_x, far_to, far_ident):
        arrived(region(block, None), gather_recv.at[ident])
        if far_to is not None:
            gsend(block, None, far_ident, far_to)
        base = 6 if along_x else 18
        up, down = (x_next, x_prev) if along_x else (z_next, z_prev)
        gsend(block, None, base + j, up)
        gsend(block, None, base + 3 + j, down)
        to_partner(block, None, ident)

    y_piece(a_prev, 0, 0, True, y_next, 4)
    y_piece(b_next, 3, 1, False, y_prev, 5)
    y_piece(a_next, 1, 1, True, None, None)
    y_piece(b_prev, 2, 0, False, None, None)
    y_piece(a_far, 4, 2, True, None, None)
    y_piece(b_far, 5, 2, False, None, None)

    shard = (s_prev, s_next, s_far)
    x_up, x_down, x_far = lax.rem(x + 3, 4), lax.rem(x + 1, 4), lax.rem(x + 2, 4)
    z_up, z_down, z_far = lax.rem(z + 3, 4), lax.rem(z + 1, 4), lax.rem(z + 2, 4)

    def ring_piece(j, along_x):
        base = 6 if along_x else 18
        off = 0 if along_x else 4
        from_prev = shard[j] * 8 + off + (x_up if along_x else z_up)
        from_next = shard[j] * 8 + off + (x_down if along_x else z_down)
        up, down = (x_next, x_prev) if along_x else (z_next, z_prev)
        arrived(region(from_prev, None), gather_recv.at[base + j])
        gsend(from_prev, 0, base + 6 + j, up)
        to_partner(from_prev, None, base + j)
        arrived(region(from_next, None), gather_recv.at[base + 3 + j])
        gsend(from_next, 1, base + 9 + j, down)
        to_partner(from_next, None, base + 3 + j)

    def far_piece(j, along_x):
        base = 6 if along_x else 18
        off = 0 if along_x else 4
        block = shard[j] * 8 + off + (x_far if along_x else z_far)
        for half in range(2):
            ident = base + 6 + 3 * half + j
            arrived(region(block, half), gather_recv.at[ident])
            to_partner(block, half, ident)

    ring_piece(0, True)
    ring_piece(1, False)
    ring_piece(1, True)
    ring_piece(0, False)
    ring_piece(2, True)
    ring_piece(2, False)

    eye = lax.broadcasted_iota(jnp.int32, (BLK, BLK), 0) == lax.broadcasted_iota(
        jnp.int32, (BLK, BLK), 1
    )
    wide = (BLK, BLK)

    def column(row):
        spread = jnp.where(eye, jnp.broadcast_to(row, wide), 0.0)
        return jnp.broadcast_to(jnp.sum(spread, axis=1, keepdims=True), wide)

    def mass_step(b, carry):
        row = run_mass[pl.ds(b, 1)]
        a_col[b] = column(row)
        loga_col[b] = column(jnp.log(row) * LOG2E)
        return carry

    lax.fori_loop(0, RB, mass_step, 0)
    onehot[...] = onehot_t[...].T.astype(BF16)

    for k in range(1, NAR):
        owner = lax.rem(n + NAR - k, NAR)
        arrived(v_all.at[pl.ds(owner * 8, 8)], start_recv.at[k])

    def pick_rows(table, to):
        def step(b, carry):
            for t in range(TOPC):
                to[pl.ds(b * TOPC + t, 1)] = table[pl.ds(cand[b, t], 1)]
            return carry

        lax.fori_loop(0, RB, step, 0)

    pick_rows(v_all, rows_a)
    alive = rows_live[...] > 0.5
    rows_a[...] = jnp.where(alive, rows_a[...] * (2.0 * LOG2E), FLOOR)

    far_piece(0, True)
    far_piece(1, False)
    far_piece(1, True)
    far_piece(0, False)
    far_piece(2, True)
    far_piece(2, False)

    other = partner[1]
    arrived(ref_all.at[pl.ds(other * 8, 8)], pair_recv.at[30])
    o_shard = tuple(s + 1 - 2 * c for s in shard)
    for j in range(3):
        pass
    pieces = []
    pieces += [(o_shard[0] * 8 + x, None, 0), (o_shard[1] * 8 + x, None, 1)]
    pieces += [(o_shard[0] * 8 + 4 + z, None, 2), (o_shard[1] * 8 + 4 + z, None, 3)]
    pieces += [(o_shard[2] * 8 + x, None, 4), (o_shard[2] * 8 + 4 + z, None, 5)]
    for j in range(3):
        for base, off, up, down, far in (
            (6, 0, x_up, x_down, x_far),
            (18, 4, z_up, z_down, z_far),
        ):
            pieces.append((o_shard[j] * 8 + off + up, None, base + j))
            pieces.append((o_shard[j] * 8 + off + down, None, base + 3 + j))
            pieces.append((o_shard[j] * 8 + off + far, 0, base + 6 + j))
            pieces.append((o_shard[j] * 8 + off + far, 1, base + 9 + j))
    for block, half, ident in pieces:
        arrived(region(block, half), pair_recv.at[ident])
    own_copy.wait()
    run_copy.wait()

    def cost_step(b, carry):
        run = run_v[b]
        top = None
        for h in range(TOPC // 2):
            e = b * TOPC + 2 * h
            both = jnp.concatenate([ref_all[cand[b, 2 * h]], ref_all[cand[b, 2 * h + 1]]], axis=0)
            prod = lax.dot_general(
                run, both, (((1,), (1,)), ((), ())), preferred_element_type=F32
            ) * (LOG2E / 8.0)
            for q in range(2):
                s = prod[:, q * BLK : (q + 1) * BLK]
                tiles[e + q] = s
                s = s + rows_a[pl.ds(e + q, 1)]
                top = s if top is None else jnp.maximum(top, s)
        r_col[b] = jnp.broadcast_to(jnp.max(top, axis=1, keepdims=True), wide)
        return carry

    lax.fori_loop(0, RB, cost_step, 0, unroll=2)

    def row_step(b, carry):
        top = r_col[b]
        total = None
        for t in range(TOPC):
            e = b * TOPC + t
            p = jnp.exp2(tiles[e] + rows_a[pl.ds(e, 1)] - top)
            total = p if total is None else total + p
        total = jnp.broadcast_to(jnp.sum(total, axis=1, keepdims=True), wide)
        u_col[b] = loga_col[b] - (top + jnp.log(total) * LOG2E)
        return carry

    lax.fori_loop(0, RB, row_step, 0, unroll=2)

    def column_step(b, carry):
        u = u_col[b]
        for t in range(TOPC):
            e = b * TOPC + t
            s = tiles[e] + u
            m = jnp.max(s, axis=0, keepdims=True)
            p = jnp.exp2(s - m)
            tiles[e] = p
            rows_m[pl.ds(e, 1)] = m
            rows_t[pl.ds(e, 1)] = jnp.sum(p, axis=0, keepdims=True)
        return carry

    lax.fori_loop(0, RB, column_step, 0, unroll=2)
    alive = rows_live[...] > 0.5
    rows_m[...] = jnp.where(alive, rows_m[...], FLOOR)
    block_id = lax.broadcasted_iota(jnp.int32, (REFB, BLK), 0)

    def peak_step(b, top):
        for t in range(TOPC):
            e = b * TOPC + t
            top = jnp.maximum(
                top, jnp.where(block_id == cand[b, t], rows_m[pl.ds(e, 1)], FLOOR)
            )
        return top

    top = lax.fori_loop(0, RB, peak_step, jnp.full((REFB, BLK), FLOOR, F32))
    peak[...] = top
    pick_rows(peak, rows_a)

    def spread(rows):
        hi = rows.astype(BF16)
        rest = rows - hi.astype(F32)
        mid = rest.astype(BF16)
        low = (rest - mid.astype(F32)).astype(BF16)
        total = None
        for piece in (hi, mid, low):
            d = lax.dot_general(
                onehot[0:REFB], piece, (((1,), (0,)), ((), ())), preferred_element_type=F32
            )
            total = d if total is None else total + d
        return total

    scaled = jnp.where(alive, rows_t[...] * jnp.exp2(rows_m[...] - rows_a[...]), 0.0)
    total = spread(scaled)
    joined = jnp.where(total > 0.0, peak[...] + jnp.log(total) * LOG2E, FLOOR)

    def log_sum(parts):
        top = parts[0]
        for p in parts[1:]:
            top = jnp.maximum(top, p)
        total = None
        for p in parts:
            e = jnp.exp2(p - top)
            total = e if total is None else total + e
        return top + jnp.log(total) * LOG2E

    def plain_sum(parts):
        total = parts[0]
        for p in parts[1:]:
            total = total + p
        return total

    def reduced(it, value, join):
        dense[it] = value
        for k in range(1, NAR):
            to = lax.rem(n + k, NAR)
            send(
                dense.at[it, pl.ds(to * 8, 8)],
                rs_buf.at[it, n],
                rs_send.at[it, k],
                rs_recv.at[it, k],
                (g, to),
            )
        rs_buf[it, n] = dense[it, pl.ds(n * 8, 8)]
        for k in range(1, NAR):
            arrived(rs_buf.at[it, lax.rem(n + NAR - k, NAR)], rs_recv.at[it, k])
        mine = join([rs_buf[it, k] for k in range(NAR)])
        part[it] = mine
        for k in range(1, GRP):
            send(
                part.at[it],
                ar_buf.at[it, g],
                ar_send.at[it, k],
                ar_recv.at[it, k],
                (lax.rem(g + k, GRP), n),
            )
        ar_buf[it, g] = mine
        for k in range(1, GRP):
            arrived(ar_buf.at[it, lax.rem(g + GRP - k, GRP)], ar_recv.at[it, k])
        return join([ar_buf[it, k] for k in range(GRP)])

    def gathered(it, value):
        final[it] = value
        for k in range(1, NAR):
            send(
                final.at[it],
                ag_buf.at[it, pl.ds(n * 8, 8)],
                ag_send.at[it, k],
                ag_recv.at[it, k],
                (g, lax.rem(n + k, NAR)),
            )
        ag_buf[it, pl.ds(n * 8, 8)] = value
        for k in range(1, NAR):
            owner = lax.rem(n + NAR - k, NAR)
            arrived(ag_buf.at[it, pl.ds(owner * 8, 8)], ag_recv.at[it, k])

    column_total = reduced(0, joined, log_sum)
    v_one = jnp.log(ref_mass[...]) * LOG2E - column_total
    gathered(0, v_one)
    pick_rows(ag_buf.at[0], rows_a)
    rows_m[...] = jnp.where(alive, jnp.exp2(rows_m[...] + rows_a[...]), 0.0)
    rows_t[...] = rows_m[...]

    def row_sums(b):
        total = None
        for t in range(TOPC):
            e = b * TOPC + t
            p = tiles[e] * rows_t[pl.ds(e, 1)]
            total = p if total is None else total + p
        return jnp.broadcast_to(jnp.sum(total, axis=1, keepdims=True), wide)

    def second_rows(b, carry):
        r_col[b] = a_col[b] / row_sums(b)
        return carry

    def third_rows(b, carry):
        alpha = a_col[b] / row_sums(b)
        r_col[b] = alpha
        u = (u_col[b] + jnp.log(alpha) * LOG2E) * (0.5 * LN2)
        out_run[pl.ds(b, 1)] = jnp.sum(jnp.where(eye, u, 0.0), axis=0, keepdims=True)
        return carry

    def columns(b, carry):
        alpha = r_col[b]
        for t in range(TOPC):
            e = b * TOPC + t
            rows_a[pl.ds(e, 1)] = jnp.sum(tiles[e] * alpha, axis=0, keepdims=True)
        return carry

    lax.fori_loop(0, RB, second_rows, 0, unroll=2)
    lax.fori_loop(0, RB, columns, 0, unroll=2)
    second = reduced(1, spread(rows_a[...] * rows_m[...]), plain_sum)
    gathered(1, ref_mass[...] / second)
    pick_rows(ag_buf.at[1], rows_a)
    rows_t[...] = rows_m[...] * rows_a[...]
    lax.fori_loop(0, RB, third_rows, 0, unroll=2)
    lax.fori_loop(0, RB, columns, 0, unroll=2)
    third = reduced(2, spread(rows_a[...] * rows_m[...]), plain_sum)
    out_ref[...] = (v_one + jnp.log(ref_mass[...] / third) * LOG2E) * (0.5 * LN2)

    for copy in sent:
        copy.wait_send()


def shards(run_desc, ref_desc, candidates, live_slots, run_mass, ref_mass, ref_start):
    vmem = pl.BlockSpec(memory_space=pltpu.VMEM)
    smem = pl.BlockSpec(memory_space=pltpu.SMEM)
    hbm = pl.BlockSpec(memory_space=pl.ANY)
    dma = pltpu.SemaphoreType.DMA
    run_potential, ref_potential = pl.pallas_call(
        kernel,
        out_shape=(
            jax.ShapeDtypeStruct((RB, BLK), F32),
            jax.ShapeDtypeStruct((8, BLK), F32),
        ),
        in_specs=[smem, smem, hbm, hbm, vmem, vmem, vmem],
        out_specs=(vmem, vmem),
        scratch_shapes=[
            pltpu.VMEM((REFB, BLK, D), BF16),
            pltpu.VMEM((RB, BLK, D), BF16),
            pltpu.VMEM((ENT, BLK, BLK), F32),
            pltpu.VMEM((REFB, BLK), F32),
            pltpu.VMEM((ENT, BLK), F32),
            pltpu.VMEM((ENT, BLK), F32),
            pltpu.VMEM((ENT, BLK), F32),
            pltpu.VMEM((ENT, BLK), F32),
            pltpu.VMEM((ENT, BLK), F32),
            pltpu.VMEM((BLK, ENT), BF16),
            pltpu.VMEM((RB, BLK, BLK), F32),
            pltpu.VMEM((RB, BLK, BLK), F32),
            pltpu.VMEM((RB, BLK, BLK), F32),
            pltpu.VMEM((RB, BLK, BLK), F32),
            pltpu.VMEM((3, REFB, BLK), F32),
            pltpu.VMEM((REFB, BLK), F32),
            pltpu.VMEM((3, NAR, 8, BLK), F32),
            pltpu.VMEM((3, 8, BLK), F32),
            pltpu.VMEM((3, GRP, 8, BLK), F32),
            pltpu.VMEM((2, 8, BLK), F32),
            pltpu.VMEM((2, REFB, BLK), F32),
            dma((2,)),
            dma((1,)),
            dma((32,)),
            dma((30,)),
            dma((31,)),
            dma((31,)),
            dma((NAR,)),
            dma((NAR,)),
            dma((3, NAR)),
            dma((3, NAR)),
            dma((3, GRP)),
            dma((3, GRP)),
            dma((2, NAR)),
            dma((2, NAR)),
        ],
        compiler_params=pltpu.CompilerParams(
            collective_id=0, has_side_effects=True, vmem_limit_bytes=56 * 1024 * 1024
        ),
        name="sinkhorn",
    )(
        candidates,
        live_slots,
        run_desc.reshape(RB, BLK, D),
        ref_desc.reshape(8, BLK, D),
        run_mass.reshape(RB, BLK),
        ref_mass.reshape(8, BLK),
        ref_start.reshape(8, BLK),
    )
    return run_potential.reshape(-1), ref_potential.reshape(-1)


def solution(mesh):
    both = P(("grp", "nar"))
    wide = P(("grp", "nar"), None)
    return jax.shard_map(
        shards,
        mesh=mesh,
        in_specs=(wide, P("nar", None), wide, both, both, P("nar"), P("nar")),
        out_specs=(both, P("nar")),
        check_vma=False,
    )
```

```python
import math

import jax
import jax.numpy as jnp
from jax import lax
from jax.experimental import pallas as pl
from jax.experimental.pallas import tpu as pltpu
from jax.sharding import PartitionSpec as P

BLK = 128
TOPC = 8
RB = 32
ENT = RB * TOPC
D = 256
REFB = 64
NAR = 8
GRP = 16
LOG2E = math.log2(math.e)
LN2 = math.log(2.0)
FLOOR = -1e30
MESH = pl.DeviceIdType.MESH
F32 = jnp.float32
BF16 = jnp.bfloat16


def kernel(
    cand,
    live,
    run_hbm,
    ref_hbm,
    run_mass,
    ref_mass,
    start,
    out_run,
    out_ref,
    ref_all,
    own_v,
    run_v,
    tiles,
    v_all,
    rows_a,
    rows_m,
    rows_t,
    rows_live,
    onehot_t,
    onehot,
    a_col,
    loga_col,
    r_col,
    u_col,
    dense,
    peak,
    rs_buf,
    part,
    ar_buf,
    final,
    ag_buf,
    local_sem,
    own_send,
    gather_send,
    gather_recv,
    pair_send,
    pair_recv,
    start_send,
    start_recv,
    rs_send,
    rs_recv,
    ar_send,
    ar_recv,
    ag_send,
    ag_recv,
):
    g = lax.axis_index("grp")
    n = lax.axis_index("nar")
    z, x = lax.div(g, 4), lax.rem(g, 4)
    y, c = lax.div(n, 2), lax.rem(n, 2)

    barrier = pltpu.get_barrier_semaphore()
    for k in range(1, NAR):
        pl.semaphore_signal(
            barrier, inc=1, device_id=(g, lax.rem(n + k, NAR)), device_id_type=MESH
        )
    for k in range(1, GRP):
        pl.semaphore_signal(
            barrier, inc=1, device_id=(lax.rem(g + k, GRP), n), device_id_type=MESH
        )

    own_copy = pltpu.make_async_copy(ref_hbm, own_v, local_sem.at[0])
    own_copy.start()
    run_copy = pltpu.make_async_copy(run_hbm, run_v, local_sem.at[1])
    run_copy.start()

    own_copy.wait()
    for k in range(8):
        ref_all[n * 8 + k] = own_v[k].T
    lane64 = lax.broadcasted_iota(jnp.int32, (1, BLK), 1)

    def table_step(b, carry):
        for t in range(TOPC):
            e = b * TOPC + t
            onehot_t[pl.ds(e, 1)] = jnp.where(lane64 == cand[t, b], 1.0, 0.0).astype(F32)
            rows_live[pl.ds(e, 1)] = jnp.where(
                jnp.full((1, BLK), t, jnp.int32) < live[b], 1.0, 0.0
            ).astype(F32)
        return carry

    lax.fori_loop(0, RB, table_step, 0)

    pl.semaphore_wait(barrier, NAR + GRP - 2)

    partner = (g, y * 2 + 1 - c)
    y_next = (g, lax.rem(y + 1, 4) * 2 + c)
    y_prev = (g, lax.rem(y + 3, 4) * 2 + c)
    x_next = (z * 4 + lax.rem(x + 1, 4), n)
    x_prev = (z * 4 + lax.rem(x + 3, 4), n)
    z_next = (lax.rem(z + 1, 4) * 4 + x, n)
    z_prev = (lax.rem(z + 3, 4) * 4 + x, n)
    s_prev = y_prev[1]
    s_next = y_next[1]
    s_far = lax.rem(y + 2, 4) * 2 + c

    sent = []

    def send(src, dst, send_sem, recv_sem, to):
        copy = pltpu.make_async_remote_copy(
            src_ref=src,
            dst_ref=dst,
            send_sem=send_sem,
            recv_sem=recv_sem,
            device_id=to,
            device_id_type=MESH,
        )
        copy.start()
        sent.append(copy)

    def arrived(dst, recv_sem):
        pltpu.make_async_remote_copy(
            src_ref=dst,
            dst_ref=dst,
            send_sem=own_send.at[0],
            recv_sem=recv_sem,
            device_id=partner,
            device_id_type=MESH,
        ).wait_recv()

    counter = [0]

    def region(block, half):
        if half is None:
            return ref_all.at[block]
        return ref_all.at[block, pl.ds(half * 128, 128)]

    def gsend(block, half, ident, to, src=None):
        dst = region(block, half)
        k = counter[0]
        counter[0] += 1
        send(dst if src is None else src, dst, gather_send.at[k], gather_recv.at[ident], to)

    def to_partner(block, half, ident):
        dst = region(block, half)
        send(dst, dst, pair_send.at[ident], pair_recv.at[ident], partner)

    own_a, own_b = n * 8 + x, n * 8 + 4 + z
    gsend(own_a, None, 0, y_next, ref_all.at[own_a])
    gsend(own_a, None, 1, y_prev, ref_all.at[own_a])
    gsend(own_b, None, 2, y_next, ref_all.at[own_b])
    gsend(own_b, None, 3, y_prev, ref_all.at[own_b])
    y_over = (g, s_far)
    x_over = (z * 4 + lax.rem(x + 2, 4), n)
    z_over = (lax.rem(z + 2, 4) * 4 + x, n)
    gsend(own_a, None, 4, y_over)
    gsend(own_b, None, 5, y_over)
    for k in range(1, NAR):
        send(
            start,
            v_all.at[pl.ds(n * 8, 8)],
            start_send.at[k],
            start_recv.at[k],
            (g, lax.rem(n + k, NAR)),
        )
    own_part = ref_all.at[pl.ds(n * 8, 8)]
    send(own_part, own_part, pair_send.at[30], pair_recv.at[30], partner)
    v_all[pl.ds(n * 8, 8)] = start[...]

    eye = lax.broadcasted_iota(jnp.int32, (BLK, BLK), 0) == lax.broadcasted_iota(
        jnp.int32, (BLK, BLK), 1
    )
    wide = (BLK, BLK)

    def column(row):
        spread = jnp.where(eye, jnp.broadcast_to(row, wide), 0.0)
        return jnp.broadcast_to(jnp.sum(spread, axis=1, keepdims=True), wide)

    def mass_step(b, carry):
        row = run_mass[pl.ds(b, 1)]
        a_col[b] = column(row)
        loga_col[b] = column(jnp.log(row) * LOG2E)
        return carry

    lax.fori_loop(0, RB, mass_step, 0)
    onehot[...] = onehot_t[...].T.astype(BF16)

    a_prev, a_next, a_far = s_prev * 8 + x, s_next * 8 + x, s_far * 8 + x
    b_prev, b_next, b_far = s_prev * 8 + 4 + z, s_next * 8 + 4 + z, s_far * 8 + 4 + z

    def y_piece(block, ident, j, along_x):
        arrived(region(block, None), gather_recv.at[ident])
        base = 6 if along_x else 18
        up, down = (x_next, x_prev) if along_x else (z_next, z_prev)
        gsend(block, None, base + j, up)
        gsend(block, None, base + 3 + j, down)
        gsend(block, None, base + 6 + j, x_over if along_x else z_over)
        to_partner(block, None, ident)

    y_piece(a_prev, 0, 0, True)
    y_piece(b_next, 3, 1, False)
    y_piece(a_next, 1, 1, True)
    y_piece(b_prev, 2, 0, False)
    y_piece(a_far, 4, 2, True)
    y_piece(b_far, 5, 2, False)

    shard = (s_prev, s_next, s_far)
    x_up, x_down, x_far = lax.rem(x + 3, 4), lax.rem(x + 1, 4), lax.rem(x + 2, 4)
    z_up, z_down, z_far = lax.rem(z + 3, 4), lax.rem(z + 1, 4), lax.rem(z + 2, 4)

    def ring_piece(j, along_x):
        base = 6 if along_x else 18
        off = 0 if along_x else 4
        from_prev = shard[j] * 8 + off + (x_up if along_x else z_up)
        from_next = shard[j] * 8 + off + (x_down if along_x else z_down)
        up, down = (x_next, x_prev) if along_x else (z_next, z_prev)
        arrived(region(from_prev, None), gather_recv.at[base + j])
        to_partner(from_prev, None, base + j)
        arrived(region(from_next, None), gather_recv.at[base + 3 + j])
        to_partner(from_next, None, base + 3 + j)

    def far_piece(j, along_x):
        base = 6 if along_x else 18
        off = 0 if along_x else 4
        block = shard[j] * 8 + off + (x_far if along_x else z_far)
        arrived(region(block, None), gather_recv.at[base + 6 + j])
        to_partner(block, None, base + 6 + j)

    ring_piece(0, True)
    ring_piece(1, False)
    ring_piece(1, True)
    ring_piece(0, False)
    ring_piece(2, True)
    ring_piece(2, False)

    for k in range(1, NAR):
        owner = lax.rem(n + NAR - k, NAR)
        arrived(v_all.at[pl.ds(owner * 8, 8)], start_recv.at[k])

    def pick_rows(table, to):
        def step(b, carry):
            for t in range(TOPC):
                to[pl.ds(b * TOPC + t, 1)] = table[pl.ds(cand[t, b], 1)]
            return carry

        lax.fori_loop(0, RB, step, 0)

    pick_rows(v_all, rows_a)
    alive = rows_live[...] > 0.5
    rows_a[...] = jnp.where(alive, rows_a[...] * (2.0 * LOG2E), FLOOR)

    far_piece(0, True)
    far_piece(1, False)
    far_piece(1, True)
    far_piece(0, False)
    far_piece(2, True)
    far_piece(2, False)

    other = partner[1]
    arrived(ref_all.at[pl.ds(other * 8, 8)], pair_recv.at[30])
    o_shard = tuple(s + 1 - 2 * c for s in shard)
    pieces = []
    pieces += [(o_shard[0] * 8 + x, None, 0), (o_shard[1] * 8 + x, None, 1)]
    pieces += [(o_shard[0] * 8 + 4 + z, None, 2), (o_shard[1] * 8 + 4 + z, None, 3)]
    pieces += [(o_shard[2] * 8 + x, None, 4), (o_shard[2] * 8 + 4 + z, None, 5)]
    for j in range(3):
        for base, off, up, down, far in (
            (6, 0, x_up, x_down, x_far),
            (18, 4, z_up, z_down, z_far),
        ):
            pieces.append((o_shard[j] * 8 + off + up, None, base + j))
            pieces.append((o_shard[j] * 8 + off + down, None, base + 3 + j))
            pieces.append((o_shard[j] * 8 + off + far, None, base + 6 + j))
    for block, half, ident in pieces:
        arrived(region(block, half), pair_recv.at[ident])
    run_copy.wait()

    def cost_step(b, carry):
        run = run_v[b]
        top = None
        for h in range(TOPC // 2):
            e = b * TOPC + 2 * h
            both = jnp.concatenate([ref_all[cand[2 * h, b]], ref_all[cand[2 * h + 1, b]]], axis=1)
            prod = lax.dot_general(
                run, both, (((1,), (0,)), ((), ())), preferred_element_type=F32
            ) * (LOG2E / 8.0)
            for q in range(2):
                s = prod[:, q * BLK : (q + 1) * BLK]
                tiles[e + q] = s
                s = s + rows_a[pl.ds(e + q, 1)]
                top = s if top is None else jnp.maximum(top, s)
        r_col[b] = jnp.broadcast_to(jnp.max(top, axis=1, keepdims=True), wide)
        return carry

    lax.fori_loop(0, RB, cost_step, 0, unroll=4)

    def row_step(b, carry):
        top = r_col[b]
        total = None
        for t in range(TOPC):
            e = b * TOPC + t
            p = jnp.exp2(tiles[e] + rows_a[pl.ds(e, 1)] - top)
            total = p if total is None else total + p
        total = jnp.broadcast_to(jnp.sum(total, axis=1, keepdims=True), wide)
        u_col[b] = loga_col[b] - (top + jnp.log(total) * LOG2E)
        return carry

    lax.fori_loop(0, RB, row_step, 0, unroll=4)

    def column_step(b, carry):
        u = u_col[b]
        for t in range(TOPC):
            e = b * TOPC + t
            s = tiles[e] + u
            m = jnp.max(s, axis=0, keepdims=True)
            p = jnp.exp2(s - m)
            tiles[e] = p
            rows_m[pl.ds(e, 1)] = m
            rows_t[pl.ds(e, 1)] = jnp.sum(p, axis=0, keepdims=True)
        return carry

    lax.fori_loop(0, RB, column_step, 0, unroll=4)
    alive = rows_live[...] > 0.5
    rows_m[...] = jnp.where(alive, rows_m[...], FLOOR)
    block_id = lax.broadcasted_iota(jnp.int32, (REFB, BLK), 0)

    def peak_step(b, top):
        for t in range(TOPC):
            e = b * TOPC + t
            top = jnp.maximum(
                top, jnp.where(block_id == cand[t, b], rows_m[pl.ds(e, 1)], FLOOR)
            )
        return top

    top = lax.fori_loop(0, RB, peak_step, jnp.full((REFB, BLK), FLOOR, F32), unroll=2)
    peak[...] = top
    pick_rows(peak, rows_a)

    def spread(rows):
        hi = rows.astype(BF16)
        rest = rows - hi.astype(F32)
        mid = rest.astype(BF16)
        low = (rest - mid.astype(F32)).astype(BF16)
        total = None
        for piece in (hi, mid, low):
            d = lax.dot_general(
                onehot[0:REFB], piece, (((1,), (0,)), ((), ())), preferred_element_type=F32
            )
            total = d if total is None else total + d
        return total

    scaled = jnp.where(alive, rows_t[...] * jnp.exp2(rows_m[...] - rows_a[...]), 0.0)
    total = spread(scaled)
    joined = jnp.where(total > 0.0, peak[...] + jnp.log(total) * LOG2E, FLOOR)

    def log_sum(parts):
        top = parts[0]
        for p in parts[1:]:
            top = jnp.maximum(top, p)
        total = None
        for p in parts:
            e = jnp.exp2(p - top)
            total = e if total is None else total + e
        return top + jnp.log(total) * LOG2E

    def plain_sum(parts):
        total = parts[0]
        for p in parts[1:]:
            total = total + p
        return total

    def reduced(it, value, join):
        dense[it] = value
        for k in range(1, NAR):
            to = lax.rem(n + k, NAR)
            send(
                dense.at[it, pl.ds(to * 8, 8)],
                rs_buf.at[it, n],
                rs_send.at[it, k],
                rs_recv.at[it, k],
                (g, to),
            )
        rs_buf[it, n] = dense[it, pl.ds(n * 8, 8)]
        for k in range(1, NAR):
            arrived(rs_buf.at[it, lax.rem(n + NAR - k, NAR)], rs_recv.at[it, k])
        mine = join([rs_buf[it, k] for k in range(NAR)])
        part[it] = mine
        for k in range(1, GRP):
            send(
                part.at[it],
                ar_buf.at[it, g],
                ar_send.at[it, k],
                ar_recv.at[it, k],
                (lax.rem(g + k, GRP), n),
            )
        ar_buf[it, g] = mine
        for k in range(1, GRP):
            arrived(ar_buf.at[it, lax.rem(g + GRP - k, GRP)], ar_recv.at[it, k])
        return join([ar_buf[it, k] for k in range(GRP)])

    def gathered(it, value):
        final[it] = value
        for k in range(1, NAR):
            send(
                final.at[it],
                ag_buf.at[it, pl.ds(n * 8, 8)],
                ag_send.at[it, k],
                ag_recv.at[it, k],
                (g, lax.rem(n + k, NAR)),
            )
        ag_buf[it, pl.ds(n * 8, 8)] = value
        for k in range(1, NAR):
            owner = lax.rem(n + NAR - k, NAR)
            arrived(ag_buf.at[it, pl.ds(owner * 8, 8)], ag_recv.at[it, k])

    column_total = reduced(0, joined, log_sum)
    v_one = jnp.log(ref_mass[...]) * LOG2E - column_total
    gathered(0, v_one)
    pick_rows(ag_buf.at[0], rows_a)
    rows_m[...] = jnp.where(alive, jnp.exp2(rows_m[...] + rows_a[...]), 0.0)
    rows_t[...] = rows_m[...]

    def row_sums(b):
        total = None
        for t in range(TOPC):
            e = b * TOPC + t
            p = tiles[e] * rows_t[pl.ds(e, 1)]
            total = p if total is None else total + p
        return jnp.broadcast_to(jnp.sum(total, axis=1, keepdims=True), wide)

    def second_rows(b, carry):
        r_col[b] = a_col[b] / row_sums(b)
        return carry

    def third_rows(b, carry):
        alpha = a_col[b] / row_sums(b)
        r_col[b] = alpha
        u = (u_col[b] + jnp.log(alpha) * LOG2E) * (0.5 * LN2)
        out_run[pl.ds(b, 1)] = jnp.sum(jnp.where(eye, u, 0.0), axis=0, keepdims=True)
        return carry

    def columns(b, carry):
        alpha = r_col[b]
        for t in range(TOPC):
            e = b * TOPC + t
            rows_a[pl.ds(e, 1)] = jnp.sum(tiles[e] * alpha, axis=0, keepdims=True)
        return carry

    lax.fori_loop(0, RB, second_rows, 0, unroll=4)
    lax.fori_loop(0, RB, columns, 0, unroll=4)
    second = reduced(1, spread(rows_a[...] * rows_m[...]), plain_sum)
    gathered(1, ref_mass[...] / second)
    pick_rows(ag_buf.at[1], rows_a)
    rows_t[...] = rows_m[...] * rows_a[...]
    lax.fori_loop(0, RB, third_rows, 0, unroll=4)
    lax.fori_loop(0, RB, columns, 0, unroll=4)
    third = reduced(2, spread(rows_a[...] * rows_m[...]), plain_sum)
    out_ref[...] = (v_one + jnp.log(ref_mass[...] / third) * LOG2E) * (0.5 * LN2)

    for copy in sent:
        copy.wait_send()


def write_out(run_in, ref_in, run_out, ref_out):
    run_out[...] = run_in[...]
    ref_out[...] = ref_in[...]


def shards(run_desc, ref_desc, candidates, live_slots, run_mass, ref_mass, ref_start):
    vmem = pl.BlockSpec(memory_space=pltpu.VMEM)
    smem = pl.BlockSpec(memory_space=pltpu.SMEM)
    hbm = pl.BlockSpec(memory_space=pl.ANY)
    dma = pltpu.SemaphoreType.DMA
    run_potential, ref_potential = pl.pallas_call(
        kernel,
        out_shape=(
            jax.ShapeDtypeStruct((RB, BLK), F32),
            jax.ShapeDtypeStruct((8, BLK), F32),
        ),
        in_specs=[smem, smem, hbm, hbm, vmem, vmem, vmem],
        out_specs=(vmem, vmem),
        scratch_shapes=[
            pltpu.VMEM((REFB, D, BLK), BF16),
            pltpu.VMEM((8, BLK, D), BF16),
            pltpu.VMEM((RB, BLK, D), BF16),
            pltpu.VMEM((ENT, BLK, BLK), F32),
            pltpu.VMEM((REFB, BLK), F32),
            pltpu.VMEM((ENT, BLK), F32),
            pltpu.VMEM((ENT, BLK), F32),
            pltpu.VMEM((ENT, BLK), F32),
            pltpu.VMEM((ENT, BLK), F32),
            pltpu.VMEM((ENT, BLK), F32),
            pltpu.VMEM((BLK, ENT), BF16),
            pltpu.VMEM((RB, BLK, BLK), F32),
            pltpu.VMEM((RB, BLK, BLK), F32),
            pltpu.VMEM((RB, BLK, BLK), F32),
            pltpu.VMEM((RB, BLK, BLK), F32),
            pltpu.VMEM((3, REFB, BLK), F32),
            pltpu.VMEM((REFB, BLK), F32),
            pltpu.VMEM((3, NAR, 8, BLK), F32),
            pltpu.VMEM((3, 8, BLK), F32),
            pltpu.VMEM((3, GRP, 8, BLK), F32),
            pltpu.VMEM((2, 8, BLK), F32),
            pltpu.VMEM((2, REFB, BLK), F32),
            dma((2,)),
            dma((1,)),
            dma((32,)),
            dma((30,)),
            dma((31,)),
            dma((31,)),
            dma((NAR,)),
            dma((NAR,)),
            dma((3, NAR)),
            dma((3, NAR)),
            dma((3, GRP)),
            dma((3, GRP)),
            dma((2, NAR)),
            dma((2, NAR)),
        ],
        compiler_params=pltpu.CompilerParams(
            collective_id=0, has_side_effects=True, vmem_limit_bytes=56 * 1024 * 1024
        ),
        name="sinkhorn",
    )(
        candidates.T,
        live_slots,
        run_desc.reshape(RB, BLK, D),
        ref_desc.reshape(8, BLK, D),
        run_mass.reshape(RB, BLK),
        ref_mass.reshape(8, BLK),
        ref_start.reshape(8, BLK),
    )
    run_potential, ref_potential = pl.pallas_call(
        write_out,
        out_shape=(
            jax.ShapeDtypeStruct((RB, BLK), F32),
            jax.ShapeDtypeStruct((8, BLK), F32),
        ),
        in_specs=[vmem, vmem],
        out_specs=(vmem, vmem),
        name="write_out",
    )(run_potential, ref_potential)
    return run_potential.reshape(-1), ref_potential.reshape(-1)


def solution(mesh):
    both = P(("grp", "nar"))
    wide = P(("grp", "nar"), None)
    return jax.shard_map(
        shards,
        mesh=mesh,
        in_specs=(wide, P("nar", None), wide, both, both, P("nar"), P("nar")),
        out_specs=(both, P("nar")),
        check_vma=False,
    )
```

```python
import math

import jax
import jax.numpy as jnp
from jax import lax
from jax.experimental import pallas as pl
from jax.experimental.pallas import tpu as pltpu
from jax.sharding import PartitionSpec as P

BLK = 128
TOPC = 8
RB = 32
ENT = RB * TOPC
D = 256
REFB = 64
NAR = 8
GRP = 16
LOG2E = math.log2(math.e)
LN2 = math.log(2.0)
FLOOR = -1e30
MESH = pl.DeviceIdType.MESH
F32 = jnp.float32
BF16 = jnp.bfloat16


def kernel(
    cand,
    live,
    run_hbm,
    ref_hbm,
    run_mass,
    ref_mass,
    start,
    out_run,
    out_ref,
    ref_all,
    own_v,
    run_v,
    tiles,
    raw,
    tops,
    us,
    v_all,
    rows_a,
    rows_m,
    rows_t,
    rows_live,
    onehot_t,
    onehot,
    a_col,
    loga_col,
    r_col,
    u_col,
    dense,
    peak,
    rs_buf,
    part,
    ar_buf,
    final,
    ag_buf,
    here_sem,
    local_sem,
    own_send,
    gather_send,
    gather_recv,
    pair_send,
    pair_recv,
    start_send,
    start_recv,
    rs_send,
    rs_recv,
    ar_send,
    ar_recv,
    ag_send,
    ag_recv,
):
    g = lax.axis_index("grp")
    n = lax.axis_index("nar")
    z, x = lax.div(g, 4), lax.rem(g, 4)
    y, c = lax.div(n, 2), lax.rem(n, 2)

    barrier = pltpu.get_barrier_semaphore()
    partner = (g, y * 2 + 1 - c)
    y_next = (g, lax.rem(y + 1, 4) * 2 + c)
    y_prev = (g, lax.rem(y + 3, 4) * 2 + c)
    x_next = (z * 4 + lax.rem(x + 1, 4), n)
    x_prev = (z * 4 + lax.rem(x + 3, 4), n)
    z_next = (lax.rem(z + 1, 4) * 4 + x, n)
    z_prev = (lax.rem(z + 3, 4) * 4 + x, n)
    y_over = (g, lax.rem(y + 2, 4) * 2 + c)
    x_over = (z * 4 + lax.rem(x + 2, 4), n)
    z_over = (lax.rem(z + 2, 4) * 4 + x, n)
    rings = (y_next, y_prev, y_over, x_next, x_prev, x_over, z_next, z_prev, z_over)
    for to in (*rings, partner):
        pl.semaphore_signal(barrier, inc=1, device_id=to, device_id_type=MESH)

    own_copy = pltpu.make_async_copy(ref_hbm, own_v, local_sem.at[0])
    own_copy.start()
    run_copy = pltpu.make_async_copy(run_hbm, run_v, local_sem.at[1])
    run_copy.start()

    own_copy.wait()
    for k in range(8):
        ref_all[n * 8 + k] = own_v[k].T
    lane64 = lax.broadcasted_iota(jnp.int32, (1, BLK), 1)

    def table_step(b, carry):
        for t in range(TOPC):
            e = b * TOPC + t
            onehot_t[pl.ds(e, 1)] = jnp.where(lane64 == cand[t, b], 1.0, 0.0).astype(F32)
            rows_live[pl.ds(e, 1)] = jnp.where(
                jnp.full((1, BLK), t, jnp.int32) < live[b], 1.0, 0.0
            ).astype(F32)
        return carry

    lax.fori_loop(0, RB, table_step, 0)

    pl.semaphore_wait(barrier, 10)
    for to in (z_next, z_prev, z_over, partner):
        pl.semaphore_signal(here_sem, inc=1, device_id=to, device_id_type=MESH)

    s_prev = y_prev[1]
    s_next = y_next[1]
    s_far = lax.rem(y + 2, 4) * 2 + c

    sent = []

    def send(src, dst, send_sem, recv_sem, to):
        copy = pltpu.make_async_remote_copy(
            src_ref=src,
            dst_ref=dst,
            send_sem=send_sem,
            recv_sem=recv_sem,
            device_id=to,
            device_id_type=MESH,
        )
        copy.start()
        sent.append(copy)

    def arrived(dst, recv_sem):
        pltpu.make_async_remote_copy(
            src_ref=dst,
            dst_ref=dst,
            send_sem=own_send.at[0],
            recv_sem=recv_sem,
            device_id=partner,
            device_id_type=MESH,
        ).wait_recv()

    counter = [0]

    def region(block, half):
        if half is None:
            return ref_all.at[block]
        return ref_all.at[block, pl.ds(half * 128, 128)]

    def gsend(block, half, ident, to, src=None):
        dst = region(block, half)
        k = counter[0]
        counter[0] += 1
        send(dst if src is None else src, dst, gather_send.at[k], gather_recv.at[ident], to)

    def to_partner(block, half, ident):
        dst = region(block, half)
        send(dst, dst, pair_send.at[ident], pair_recv.at[ident], partner)

    own_a, own_b = n * 8 + x, n * 8 + 4 + z
    gsend(own_a, None, 0, y_next, ref_all.at[own_a])
    gsend(own_a, None, 1, y_prev, ref_all.at[own_a])
    gsend(own_b, None, 2, y_next, ref_all.at[own_b])
    gsend(own_b, None, 3, y_prev, ref_all.at[own_b])
    gsend(own_a, None, 4, y_over)
    gsend(own_b, None, 5, y_over)
    own_part = ref_all.at[pl.ds(n * 8, 8)]
    send(own_part, own_part, pair_send.at[30], pair_recv.at[30], partner)
    v_all[pl.ds(n * 8, 8)] = start[...]

    eye = lax.broadcasted_iota(jnp.int32, (BLK, BLK), 0) == lax.broadcasted_iota(
        jnp.int32, (BLK, BLK), 1
    )
    wide = (BLK, BLK)

    def column(row):
        spread = jnp.where(eye, jnp.broadcast_to(row, wide), 0.0)
        return jnp.broadcast_to(jnp.sum(spread, axis=1, keepdims=True), wide)

    def mass_step(b, carry):
        row = run_mass[pl.ds(b, 1)]
        a_col[b] = column(row)
        loga_col[b] = column(jnp.log(row) * LOG2E)
        return carry

    lax.fori_loop(0, RB, mass_step, 0)
    onehot[...] = onehot_t[...].T.astype(BF16)

    pl.semaphore_wait(here_sem, 4)
    for k in range(1, NAR):
        send(
            start,
            v_all.at[pl.ds(n * 8, 8)],
            start_send.at[k],
            start_recv.at[k],
            (g, lax.rem(n + k, NAR)),
        )

    a_prev, a_next, a_far = s_prev * 8 + x, s_next * 8 + x, s_far * 8 + x
    b_prev, b_next, b_far = s_prev * 8 + 4 + z, s_next * 8 + 4 + z, s_far * 8 + 4 + z

    def y_piece(block, ident, j, along_x):
        arrived(region(block, None), gather_recv.at[ident])
        base = 6 if along_x else 18
        up, down = (x_next, x_prev) if along_x else (z_next, z_prev)
        gsend(block, None, base + j, up)
        gsend(block, None, base + 3 + j, down)
        gsend(block, None, base + 6 + j, x_over if along_x else z_over)
        to_partner(block, None, ident)

    y_piece(a_prev, 0, 0, True)
    y_piece(b_next, 3, 1, False)
    y_piece(a_next, 1, 1, True)
    y_piece(b_prev, 2, 0, False)
    y_piece(a_far, 4, 2, True)
    y_piece(b_far, 5, 2, False)

    shard = (s_prev, s_next, s_far)
    x_up, x_down, x_far = lax.rem(x + 3, 4), lax.rem(x + 1, 4), lax.rem(x + 2, 4)
    z_up, z_down, z_far = lax.rem(z + 3, 4), lax.rem(z + 1, 4), lax.rem(z + 2, 4)

    def ring_piece(j, along_x):
        base = 6 if along_x else 18
        off = 0 if along_x else 4
        from_prev = shard[j] * 8 + off + (x_up if along_x else z_up)
        from_next = shard[j] * 8 + off + (x_down if along_x else z_down)
        up, down = (x_next, x_prev) if along_x else (z_next, z_prev)
        arrived(region(from_prev, None), gather_recv.at[base + j])
        to_partner(from_prev, None, base + j)
        arrived(region(from_next, None), gather_recv.at[base + 3 + j])
        to_partner(from_next, None, base + 3 + j)

    def far_piece(j, along_x):
        base = 6 if along_x else 18
        off = 0 if along_x else 4
        block = shard[j] * 8 + off + (x_far if along_x else z_far)
        arrived(region(block, None), gather_recv.at[base + 6 + j])
        to_partner(block, None, base + 6 + j)

    ring_piece(0, True)
    ring_piece(1, False)
    ring_piece(1, True)
    ring_piece(0, False)
    ring_piece(2, True)
    ring_piece(2, False)

    for k in range(1, NAR):
        owner = lax.rem(n + NAR - k, NAR)
        arrived(v_all.at[pl.ds(owner * 8, 8)], start_recv.at[k])

    def pick_rows(table, to):
        def step(b, carry):
            for t in range(TOPC):
                to[pl.ds(b * TOPC + t, 1)] = table[pl.ds(cand[t, b], 1)]
            return carry

        lax.fori_loop(0, RB, step, 0)

    pick_rows(v_all, rows_a)
    alive = rows_live[...] > 0.5
    rows_a[...] = jnp.where(alive, rows_a[...] * (2.0 * LOG2E), FLOOR)

    far_piece(0, True)
    far_piece(1, False)
    far_piece(1, True)
    far_piece(0, False)
    far_piece(2, True)
    far_piece(2, False)

    other = partner[1]
    arrived(ref_all.at[pl.ds(other * 8, 8)], pair_recv.at[30])
    o_shard = tuple(s + 1 - 2 * c for s in shard)
    pieces = []
    pieces += [(o_shard[0] * 8 + x, None, 0), (o_shard[1] * 8 + x, None, 1)]
    pieces += [(o_shard[0] * 8 + 4 + z, None, 2), (o_shard[1] * 8 + 4 + z, None, 3)]
    pieces += [(o_shard[2] * 8 + x, None, 4), (o_shard[2] * 8 + 4 + z, None, 5)]
    for j in range(3):
        for base, off, up, down, far in (
            (6, 0, x_up, x_down, x_far),
            (18, 4, z_up, z_down, z_far),
        ):
            pieces.append((o_shard[j] * 8 + off + up, None, base + j))
            pieces.append((o_shard[j] * 8 + off + down, None, base + 3 + j))
            pieces.append((o_shard[j] * 8 + off + far, None, base + 6 + j))
    for block, half, ident in pieces:
        arrived(region(block, half), pair_recv.at[ident])
    run_copy.wait()

    def cost_part(b, slot, h, top):
        both = jnp.concatenate([ref_all[cand[2 * h, b]], ref_all[cand[2 * h + 1, b]]], axis=1)
        prod = lax.dot_general(
            run_v[b], both, (((1,), (0,)), ((), ())), preferred_element_type=F32
        ) * (LOG2E / 8.0)
        for q in range(2):
            s = prod[:, q * BLK : (q + 1) * BLK]
            raw[slot][2 * h + q] = s
            s = s + rows_a[pl.ds(b * TOPC + 2 * h + q, 1)]
            top = s if top is None else jnp.maximum(top, s)
        return top

    def cost_end(slot, top):
        tops[slot][...] = jnp.broadcast_to(jnp.max(top, axis=1, keepdims=True), wide)

    def row_part(b, slot, h, total):
        for t in (2 * h, 2 * h + 1):
            p = jnp.exp2(raw[slot][t] + rows_a[pl.ds(b * TOPC + t, 1)] - tops[slot][...])
            total = p if total is None else total + p
        return total

    def row_end(b, slot, total):
        total = jnp.broadcast_to(jnp.sum(total, axis=1, keepdims=True), wide)
        u = loga_col[b] - (tops[slot][...] + jnp.log(total) * LOG2E)
        u_col[b] = u
        us[slot][...] = u

    def column_part(b, slot, h):
        for t in (2 * h, 2 * h + 1):
            e = b * TOPC + t
            s = raw[slot][t] + us[slot][...]
            m = jnp.max(s, axis=0, keepdims=True)
            p = jnp.exp2(s - m)
            tiles[e] = p
            rows_m[pl.ds(e, 1)] = m
            rows_t[pl.ds(e, 1)] = jnp.sum(p, axis=0, keepdims=True)

    def stage(b, at, cost=True, row=True, col=True):
        top = total = None
        for h in range(TOPC // 2):
            if col:
                column_part(b - 2, (at + 2) % 4, h)
            if row:
                total = row_part(b - 1, (at + 3) % 4, h, total)
            if cost:
                top = cost_part(b, at, h, top)
        if row:
            row_end(b - 1, (at + 3) % 4, total)
        if cost:
            cost_end(at, top)

    stage(0, 0, row=False, col=False)
    stage(1, 1, col=False)

    def first_step(k, carry):
        for q in range(4):
            stage(2 + 4 * k + q, (2 + q) % 4)
        return carry

    lax.fori_loop(0, 28 // 4, first_step, 0)
    stage(30, 2)
    stage(31, 3)
    stage(32, 0, cost=False)
    stage(33, 1, cost=False, row=False)
    alive = rows_live[...] > 0.5
    rows_m[...] = jnp.where(alive, rows_m[...], FLOOR)
    block_id = lax.broadcasted_iota(jnp.int32, (REFB, BLK), 0)

    def peak_step(b, top):
        for t in range(TOPC):
            e = b * TOPC + t
            top = jnp.maximum(
                top, jnp.where(block_id == cand[t, b], rows_m[pl.ds(e, 1)], FLOOR)
            )
        return top

    top = lax.fori_loop(0, RB, peak_step, jnp.full((REFB, BLK), FLOOR, F32), unroll=2)
    peak[...] = top
    pick_rows(peak, rows_a)

    def spread(rows):
        hi = rows.astype(BF16)
        rest = rows - hi.astype(F32)
        mid = rest.astype(BF16)
        low = (rest - mid.astype(F32)).astype(BF16)
        total = None
        for piece in (hi, mid, low):
            d = lax.dot_general(
                onehot[0:REFB], piece, (((1,), (0,)), ((), ())), preferred_element_type=F32
            )
            total = d if total is None else total + d
        return total

    scaled = jnp.where(alive, rows_t[...] * jnp.exp2(rows_m[...] - rows_a[...]), 0.0)
    total = spread(scaled)
    joined = jnp.where(total > 0.0, peak[...] + jnp.log(total) * LOG2E, FLOOR)

    def log_sum(parts):
        top = parts[0]
        for p in parts[1:]:
            top = jnp.maximum(top, p)
        total = None
        for p in parts:
            e = jnp.exp2(p - top)
            total = e if total is None else total + e
        return top + jnp.log(total) * LOG2E

    def plain_sum(parts):
        total = parts[0]
        for p in parts[1:]:
            total = total + p
        return total

    def reduced(it, value, join, meanwhile=None):
        dense[it] = value
        for k in range(1, NAR):
            to = lax.rem(n + k, NAR)
            send(
                dense.at[it, pl.ds(to * 8, 8)],
                rs_buf.at[it, n],
                rs_send.at[it, k],
                rs_recv.at[it, k],
                (g, to),
            )
        rs_buf[it, n] = dense[it, pl.ds(n * 8, 8)]
        if meanwhile is not None:
            meanwhile()
        for k in range(1, NAR):
            arrived(rs_buf.at[it, lax.rem(n + NAR - k, NAR)], rs_recv.at[it, k])
        mine = join([rs_buf[it, k] for k in range(NAR)])
        part[it] = mine
        for k in range(1, GRP):
            send(
                part.at[it],
                ar_buf.at[it, g],
                ar_send.at[it, k],
                ar_recv.at[it, k],
                (lax.rem(g + k, GRP), n),
            )
        ar_buf[it, g] = mine
        for k in range(1, GRP):
            arrived(ar_buf.at[it, lax.rem(g + GRP - k, GRP)], ar_recv.at[it, k])
        return join([ar_buf[it, k] for k in range(GRP)])

    def gathered(it, value):
        final[it] = value
        for k in range(1, NAR):
            send(
                final.at[it],
                ag_buf.at[it, pl.ds(n * 8, 8)],
                ag_send.at[it, k],
                ag_recv.at[it, k],
                (g, lax.rem(n + k, NAR)),
            )
        ag_buf[it, pl.ds(n * 8, 8)] = value
        for k in range(1, NAR):
            owner = lax.rem(n + NAR - k, NAR)
            arrived(ag_buf.at[it, pl.ds(owner * 8, 8)], ag_recv.at[it, k])

    column_total = reduced(0, joined, log_sum)
    v_one = jnp.log(ref_mass[...]) * LOG2E - column_total
    gathered(0, v_one)
    pick_rows(ag_buf.at[0], rows_a)
    rows_m[...] = jnp.where(alive, jnp.exp2(rows_m[...] + rows_a[...]), 0.0)
    rows_t[...] = rows_m[...]

    def row_sums(b):
        total = None
        for t in range(TOPC):
            e = b * TOPC + t
            p = tiles[e] * rows_t[pl.ds(e, 1)]
            total = p if total is None else total + p
        return jnp.broadcast_to(jnp.sum(total, axis=1, keepdims=True), wide)

    def scale_rows(b, carry):
        r_col[b] = a_col[b] / row_sums(b)
        return carry

    def run_output(b, carry):
        u = (u_col[b] + jnp.log(r_col[b]) * LOG2E) * (0.5 * LN2)
        out_run[pl.ds(b, 1)] = jnp.sum(jnp.where(eye, u, 0.0), axis=0, keepdims=True)
        return carry

    def columns(b, carry):
        alpha = r_col[b]
        for t in range(TOPC):
            e = b * TOPC + t
            rows_a[pl.ds(e, 1)] = jnp.sum(tiles[e] * alpha, axis=0, keepdims=True)
        return carry

    lax.fori_loop(0, RB, scale_rows, 0, unroll=4)
    lax.fori_loop(0, RB, columns, 0, unroll=4)
    second = reduced(1, spread(rows_a[...] * rows_m[...]), plain_sum)
    gathered(1, ref_mass[...] / second)
    pick_rows(ag_buf.at[1], rows_a)
    rows_t[...] = rows_m[...] * rows_a[...]
    lax.fori_loop(0, RB, scale_rows, 0, unroll=4)
    lax.fori_loop(0, RB, columns, 0, unroll=4)
    third = reduced(
        2,
        spread(rows_a[...] * rows_m[...]),
        plain_sum,
        lambda: lax.fori_loop(0, RB, run_output, 0, unroll=2),
    )
    out_ref[...] = (v_one + jnp.log(ref_mass[...] / third) * LOG2E) * (0.5 * LN2)

    for copy in sent:
        copy.wait_send()


def write_out(run_in, ref_in, run_out, ref_out):
    run_out[...] = run_in[...]
    ref_out[...] = ref_in[...]


def shards(run_desc, ref_desc, candidates, live_slots, run_mass, ref_mass, ref_start):
    vmem = pl.BlockSpec(memory_space=pltpu.VMEM)
    smem = pl.BlockSpec(memory_space=pltpu.SMEM)
    hbm = pl.BlockSpec(memory_space=pl.ANY)
    dma = pltpu.SemaphoreType.DMA
    run_potential, ref_potential = pl.pallas_call(
        kernel,
        out_shape=(
            jax.ShapeDtypeStruct((RB, BLK), F32),
            jax.ShapeDtypeStruct((8, BLK), F32),
        ),
        in_specs=[smem, smem, hbm, hbm, vmem, vmem, vmem],
        out_specs=(vmem, vmem),
        scratch_shapes=[
            pltpu.VMEM((REFB, D, BLK), BF16),
            pltpu.VMEM((8, BLK, D), BF16),
            pltpu.VMEM((RB, BLK, D), BF16),
            pltpu.VMEM((ENT, BLK, BLK), F32),
            [pltpu.VMEM((TOPC, BLK, BLK), F32)] * 4,
            [pltpu.VMEM((BLK, BLK), F32)] * 4,
            [pltpu.VMEM((BLK, BLK), F32)] * 4,
            pltpu.VMEM((REFB, BLK), F32),
            pltpu.VMEM((ENT, BLK), F32),
            pltpu.VMEM((ENT, BLK), F32),
            pltpu.VMEM((ENT, BLK), F32),
            pltpu.VMEM((ENT, BLK), F32),
            pltpu.VMEM((ENT, BLK), F32),
            pltpu.VMEM((BLK, ENT), BF16),
            pltpu.VMEM((RB, BLK, BLK), F32),
            pltpu.VMEM((RB, BLK, BLK), F32),
            pltpu.VMEM((RB, BLK, BLK), F32),
            pltpu.VMEM((RB, BLK, BLK), F32),
            pltpu.VMEM((3, REFB, BLK), F32),
            pltpu.VMEM((REFB, BLK), F32),
            pltpu.VMEM((3, NAR, 8, BLK), F32),
            pltpu.VMEM((3, 8, BLK), F32),
            pltpu.VMEM((3, GRP, 8, BLK), F32),
            pltpu.VMEM((2, 8, BLK), F32),
            pltpu.VMEM((2, REFB, BLK), F32),
            pltpu.SemaphoreType.REGULAR,
            dma((2,)),
            dma((1,)),
            dma((32,)),
            dma((30,)),
            dma((31,)),
            dma((31,)),
            dma((NAR,)),
            dma((NAR,)),
            dma((3, NAR)),
            dma((3, NAR)),
            dma((3, GRP)),
            dma((3, GRP)),
            dma((2, NAR)),
            dma((2, NAR)),
        ],
        compiler_params=pltpu.CompilerParams(
            collective_id=0, has_side_effects=True, vmem_limit_bytes=56 * 1024 * 1024
        ),
        name="sinkhorn",
    )(
        candidates.T,
        live_slots,
        run_desc.reshape(RB, BLK, D),
        ref_desc.reshape(8, BLK, D),
        run_mass.reshape(RB, BLK),
        ref_mass.reshape(8, BLK),
        ref_start.reshape(8, BLK),
    )
    run_potential, ref_potential = pl.pallas_call(
        write_out,
        out_shape=(
            jax.ShapeDtypeStruct((RB, BLK), F32),
            jax.ShapeDtypeStruct((8, BLK), F32),
        ),
        in_specs=[vmem, vmem],
        out_specs=(vmem, vmem),
        name="write_out",
    )(run_potential, ref_potential)
    return run_potential.reshape(-1), ref_potential.reshape(-1)


def solution(mesh):
    both = P(("grp", "nar"))
    wide = P(("grp", "nar"), None)
    return jax.shard_map(
        shards,
        mesh=mesh,
        in_specs=(wide, P("nar", None), wide, both, both, P("nar"), P("nar")),
        out_specs=(both, P("nar")),
        check_vma=False,
    )
```

```python
import math

import jax
import jax.numpy as jnp
from jax import lax
from jax.experimental import pallas as pl
from jax.experimental.pallas import tpu as pltpu
from jax.sharding import PartitionSpec as P

BLK = 128
TOPC = 8
RB = 32
ENT = RB * TOPC
D = 256
REFB = 64
NAR = 8
GRP = 16
LOG2E = math.log2(math.e)
LN2 = math.log(2.0)
FLOOR = -1e30
MESH = pl.DeviceIdType.MESH
F32 = jnp.float32
BF16 = jnp.bfloat16


def kernel(
    cand_in,
    live_in,
    run_hbm,
    ref_hbm,
    run_mass_in,
    ref_mass_in,
    start_in,
    out_run,
    out_ref,
    cand,
    live,
    run_mass,
    ref_mass,
    start,
    ref_all,
    own_v,
    run_v,
    tiles,
    raw,
    tops,
    us,
    v_all,
    rows_a,
    rows_m,
    rows_t,
    rows_live,
    onehot_t,
    onehot,
    a_col,
    loga_col,
    r_col,
    u_col,
    dense,
    peak,
    rs_buf,
    part,
    ar_buf,
    final,
    ag_buf,
    here_sem,
    local_sem,
    own_send,
    gather_send,
    gather_recv,
    pair_send,
    pair_recv,
    start_send,
    start_recv,
    rs_send,
    rs_recv,
    ar_send,
    ar_recv,
    ag_send,
    ag_recv,
):
    g = lax.axis_index("grp")
    n = lax.axis_index("nar")
    z, x = lax.div(g, 4), lax.rem(g, 4)
    y, c = lax.div(n, 2), lax.rem(n, 2)

    barrier = pltpu.get_barrier_semaphore()
    partner = (g, y * 2 + 1 - c)
    y_next = (g, lax.rem(y + 1, 4) * 2 + c)
    y_prev = (g, lax.rem(y + 3, 4) * 2 + c)
    x_next = (z * 4 + lax.rem(x + 1, 4), n)
    x_prev = (z * 4 + lax.rem(x + 3, 4), n)
    z_next = (lax.rem(z + 1, 4) * 4 + x, n)
    z_prev = (lax.rem(z + 3, 4) * 4 + x, n)
    y_over = (g, lax.rem(y + 2, 4) * 2 + c)
    x_over = (z * 4 + lax.rem(x + 2, 4), n)
    z_over = (lax.rem(z + 2, 4) * 4 + x, n)
    rings = (y_next, y_prev, y_over, x_next, x_prev, x_over, z_next, z_prev, z_over)
    for to in (*rings, partner):
        pl.semaphore_signal(barrier, inc=1, device_id=to, device_id_type=MESH)

    own_copy = pltpu.make_async_copy(ref_hbm, own_v, local_sem.at[0])
    own_copy.start()
    small = [
        pltpu.make_async_copy(src, dst, local_sem.at[2 + k])
        for k, (src, dst) in enumerate(
            (
                (cand_in, cand),
                (live_in, live),
                (start_in, start),
                (run_mass_in, run_mass),
                (ref_mass_in, ref_mass),
            )
        )
    ]
    for copy in small:
        copy.start()
    run_copy = pltpu.make_async_copy(run_hbm, run_v, local_sem.at[1])
    run_copy.start()

    for copy in small:
        copy.wait()
    own_copy.wait()
    for k in range(8):
        ref_all[n * 8 + k] = own_v[k].T
    lane64 = lax.broadcasted_iota(jnp.int32, (1, BLK), 1)

    def table_step(b, carry):
        for t in range(TOPC):
            e = b * TOPC + t
            onehot_t[pl.ds(e, 1)] = jnp.where(lane64 == cand[t, b], 1.0, 0.0).astype(F32)
            rows_live[pl.ds(e, 1)] = jnp.where(
                jnp.full((1, BLK), t, jnp.int32) < live[b], 1.0, 0.0
            ).astype(F32)
        return carry

    lax.fori_loop(0, RB, table_step, 0, unroll=2)

    pl.semaphore_wait(barrier, 10)
    for to in (z_next, z_prev, z_over, partner):
        pl.semaphore_signal(here_sem, inc=1, device_id=to, device_id_type=MESH)

    s_prev = y_prev[1]
    s_next = y_next[1]
    s_far = lax.rem(y + 2, 4) * 2 + c

    sent = []

    def send(src, dst, send_sem, recv_sem, to):
        copy = pltpu.make_async_remote_copy(
            src_ref=src,
            dst_ref=dst,
            send_sem=send_sem,
            recv_sem=recv_sem,
            device_id=to,
            device_id_type=MESH,
        )
        copy.start()
        sent.append(copy)

    def arrived(dst, recv_sem):
        pltpu.make_async_remote_copy(
            src_ref=dst,
            dst_ref=dst,
            send_sem=own_send.at[0],
            recv_sem=recv_sem,
            device_id=partner,
            device_id_type=MESH,
        ).wait_recv()

    counter = [0]

    def region(block, half):
        if half is None:
            return ref_all.at[block]
        return ref_all.at[block, pl.ds(half * 128, 128)]

    def gsend(block, half, ident, to, src=None):
        dst = region(block, half)
        k = counter[0]
        counter[0] += 1
        send(dst if src is None else src, dst, gather_send.at[k], gather_recv.at[ident], to)

    def to_partner(block, half, ident):
        dst = region(block, half)
        send(dst, dst, pair_send.at[ident], pair_recv.at[ident], partner)

    own_a, own_b = n * 8 + x, n * 8 + 4 + z
    gsend(own_a, None, 0, y_next, ref_all.at[own_a])
    gsend(own_a, None, 1, y_prev, ref_all.at[own_a])
    gsend(own_b, None, 2, y_next, ref_all.at[own_b])
    gsend(own_b, None, 3, y_prev, ref_all.at[own_b])
    gsend(own_a, None, 4, y_over)
    gsend(own_b, None, 5, y_over)
    own_part = ref_all.at[pl.ds(n * 8, 8)]
    send(own_part, own_part, pair_send.at[30], pair_recv.at[30], partner)
    v_all[pl.ds(n * 8, 8)] = start[...]

    eye = lax.broadcasted_iota(jnp.int32, (BLK, BLK), 0) == lax.broadcasted_iota(
        jnp.int32, (BLK, BLK), 1
    )
    wide = (BLK, BLK)

    def column(row):
        spread = jnp.where(eye, jnp.broadcast_to(row, wide), 0.0)
        return jnp.broadcast_to(jnp.sum(spread, axis=1, keepdims=True), wide)

    def mass_step(b, carry):
        row = run_mass[pl.ds(b, 1)]
        a_col[b] = column(row)
        loga_col[b] = column(jnp.log(row) * LOG2E)
        return carry

    lax.fori_loop(0, RB, mass_step, 0)
    onehot[...] = onehot_t[...].T.astype(BF16)

    pl.semaphore_wait(here_sem, 4)
    for k in range(1, NAR):
        send(
            start,
            v_all.at[pl.ds(n * 8, 8)],
            start_send.at[k],
            start_recv.at[k],
            (g, lax.rem(n + k, NAR)),
        )

    a_prev, a_next, a_far = s_prev * 8 + x, s_next * 8 + x, s_far * 8 + x
    b_prev, b_next, b_far = s_prev * 8 + 4 + z, s_next * 8 + 4 + z, s_far * 8 + 4 + z

    def y_piece(block, ident, j, along_x):
        arrived(region(block, None), gather_recv.at[ident])
        base = 6 if along_x else 18
        up, down = (x_next, x_prev) if along_x else (z_next, z_prev)
        gsend(block, None, base + j, up)
        gsend(block, None, base + 3 + j, down)
        gsend(block, None, base + 6 + j, x_over if along_x else z_over)
        to_partner(block, None, ident)

    y_piece(a_prev, 0, 0, True)
    y_piece(b_next, 3, 1, False)
    y_piece(a_next, 1, 1, True)
    y_piece(b_prev, 2, 0, False)
    y_piece(a_far, 4, 2, True)
    y_piece(b_far, 5, 2, False)

    shard = (s_prev, s_next, s_far)
    x_up, x_down, x_far = lax.rem(x + 3, 4), lax.rem(x + 1, 4), lax.rem(x + 2, 4)
    z_up, z_down, z_far = lax.rem(z + 3, 4), lax.rem(z + 1, 4), lax.rem(z + 2, 4)

    def ring_piece(j, along_x):
        base = 6 if along_x else 18
        off = 0 if along_x else 4
        from_prev = shard[j] * 8 + off + (x_up if along_x else z_up)
        from_next = shard[j] * 8 + off + (x_down if along_x else z_down)
        up, down = (x_next, x_prev) if along_x else (z_next, z_prev)
        arrived(region(from_prev, None), gather_recv.at[base + j])
        to_partner(from_prev, None, base + j)
        arrived(region(from_next, None), gather_recv.at[base + 3 + j])
        to_partner(from_next, None, base + 3 + j)

    def far_piece(j, along_x):
        base = 6 if along_x else 18
        off = 0 if along_x else 4
        block = shard[j] * 8 + off + (x_far if along_x else z_far)
        arrived(region(block, None), gather_recv.at[base + 6 + j])
        to_partner(block, None, base + 6 + j)

    ring_piece(0, True)
    ring_piece(1, False)
    ring_piece(1, True)
    ring_piece(0, False)
    ring_piece(2, True)
    ring_piece(2, False)

    far_piece(0, True)
    far_piece(1, False)
    far_piece(1, True)
    far_piece(0, False)
    far_piece(2, True)
    far_piece(2, False)

    for k in range(1, NAR):
        owner = lax.rem(n + NAR - k, NAR)
        arrived(v_all.at[pl.ds(owner * 8, 8)], start_recv.at[k])

    def pick_rows(table, to):
        def step(b, carry):
            for t in range(TOPC):
                to[pl.ds(b * TOPC + t, 1)] = table[pl.ds(cand[t, b], 1)]
            return carry

        lax.fori_loop(0, RB, step, 0, unroll=4)

    pick_rows(v_all, rows_a)
    alive = rows_live[...] > 0.5
    rows_a[...] = jnp.where(alive, rows_a[...] * (2.0 * LOG2E), FLOOR)

    other = partner[1]
    arrived(ref_all.at[pl.ds(other * 8, 8)], pair_recv.at[30])
    o_shard = tuple(s + 1 - 2 * c for s in shard)
    pieces = []
    pieces += [(o_shard[0] * 8 + x, None, 0), (o_shard[1] * 8 + x, None, 1)]
    pieces += [(o_shard[0] * 8 + 4 + z, None, 2), (o_shard[1] * 8 + 4 + z, None, 3)]
    pieces += [(o_shard[2] * 8 + x, None, 4), (o_shard[2] * 8 + 4 + z, None, 5)]
    for j in range(3):
        for base, off, up, down, far in (
            (6, 0, x_up, x_down, x_far),
            (18, 4, z_up, z_down, z_far),
        ):
            pieces.append((o_shard[j] * 8 + off + up, None, base + j))
            pieces.append((o_shard[j] * 8 + off + down, None, base + 3 + j))
            pieces.append((o_shard[j] * 8 + off + far, None, base + 6 + j))
    for block, half, ident in pieces:
        arrived(region(block, half), pair_recv.at[ident])
    run_copy.wait()

    def cost_part(b, slot, h, top):
        both = jnp.concatenate([ref_all[cand[2 * h, b]], ref_all[cand[2 * h + 1, b]]], axis=1)
        prod = lax.dot_general(
            run_v[b], both, (((1,), (0,)), ((), ())), preferred_element_type=F32
        ) * (LOG2E / 8.0)
        for q in range(2):
            s = prod[:, q * BLK : (q + 1) * BLK]
            raw[slot][2 * h + q] = s
            s = s + rows_a[pl.ds(b * TOPC + 2 * h + q, 1)]
            top = s if top is None else jnp.maximum(top, s)
        return top

    def cost_end(slot, top):
        tops[slot][...] = jnp.broadcast_to(jnp.max(top, axis=1, keepdims=True), wide)

    def row_part(b, slot, h, total):
        for t in (2 * h, 2 * h + 1):
            p = jnp.exp2(raw[slot][t] + rows_a[pl.ds(b * TOPC + t, 1)] - tops[slot][...])
            total = p if total is None else total + p
        return total

    def row_end(b, slot, total):
        total = jnp.broadcast_to(jnp.sum(total, axis=1, keepdims=True), wide)
        u = loga_col[b] - (tops[slot][...] + jnp.log(total) * LOG2E)
        u_col[b] = u
        us[slot][...] = u

    def column_part(b, slot, h):
        for t in (2 * h, 2 * h + 1):
            e = b * TOPC + t
            s = raw[slot][t] + us[slot][...]
            m = jnp.max(s, axis=0, keepdims=True)
            p = jnp.exp2(s - m)
            tiles[e] = p
            rows_m[pl.ds(e, 1)] = m
            rows_t[pl.ds(e, 1)] = jnp.sum(p, axis=0, keepdims=True)

    def stage(b, at, cost=True, row=True, col=True):
        top = total = None
        for h in range(TOPC // 2):
            if col:
                column_part(b - 2, (at + 2) % 4, h)
            if row:
                total = row_part(b - 1, (at + 3) % 4, h, total)
            if cost:
                top = cost_part(b, at, h, top)
        if row:
            row_end(b - 1, (at + 3) % 4, total)
        if cost:
            cost_end(at, top)

    stage(0, 0, row=False, col=False)
    stage(1, 1, col=False)

    def first_step(k, carry):
        for q in range(4):
            stage(2 + 4 * k + q, (2 + q) % 4)
        return carry

    lax.fori_loop(0, 28 // 4, first_step, 0)
    stage(30, 2)
    stage(31, 3)
    stage(32, 0, cost=False)
    stage(33, 1, cost=False, row=False)
    alive = rows_live[...] > 0.5
    rows_m[...] = jnp.where(alive, rows_m[...], FLOOR)
    block_id = lax.broadcasted_iota(jnp.int32, (REFB, BLK), 0)

    def peak_step(b, top):
        for t in range(TOPC):
            e = b * TOPC + t
            top = jnp.maximum(
                top, jnp.where(block_id == cand[t, b], rows_m[pl.ds(e, 1)], FLOOR)
            )
        return top

    top = lax.fori_loop(0, RB, peak_step, jnp.full((REFB, BLK), FLOOR, F32), unroll=2)
    peak[...] = top
    pick_rows(peak, rows_a)

    def spread(rows):
        hi = rows.astype(BF16)
        rest = rows - hi.astype(F32)
        mid = rest.astype(BF16)
        low = (rest - mid.astype(F32)).astype(BF16)
        total = None
        for piece in (hi, mid, low):
            d = lax.dot_general(
                onehot[0:REFB], piece, (((1,), (0,)), ((), ())), preferred_element_type=F32
            )
            total = d if total is None else total + d
        return total

    scaled = jnp.where(alive, rows_t[...] * jnp.exp2(rows_m[...] - rows_a[...]), 0.0)
    total = spread(scaled)
    joined = jnp.where(total > 0.0, peak[...] + jnp.log(total) * LOG2E, FLOOR)

    def log_sum(parts):
        top = parts[0]
        for p in parts[1:]:
            top = jnp.maximum(top, p)
        total = None
        for p in parts:
            e = jnp.exp2(p - top)
            total = e if total is None else total + e
        return top + jnp.log(total) * LOG2E

    def plain_sum(parts):
        total = parts[0]
        for p in parts[1:]:
            total = total + p
        return total

    def reduced(it, value, join, meanwhile=None):
        dense[it] = value
        for k in range(1, NAR):
            to = lax.rem(n + k, NAR)
            send(
                dense.at[it, pl.ds(to * 8, 8)],
                rs_buf.at[it, n],
                rs_send.at[it, k],
                rs_recv.at[it, k],
                (g, to),
            )
        rs_buf[it, n] = dense[it, pl.ds(n * 8, 8)]
        if meanwhile is not None:
            meanwhile()
        for k in range(1, NAR):
            arrived(rs_buf.at[it, lax.rem(n + NAR - k, NAR)], rs_recv.at[it, k])
        mine = join([rs_buf[it, k] for k in range(NAR)])
        part[it] = mine
        for k in range(1, GRP):
            send(
                part.at[it],
                ar_buf.at[it, g],
                ar_send.at[it, k],
                ar_recv.at[it, k],
                (lax.rem(g + k, GRP), n),
            )
        ar_buf[it, g] = mine
        for k in range(1, GRP):
            arrived(ar_buf.at[it, lax.rem(g + GRP - k, GRP)], ar_recv.at[it, k])
        return join([ar_buf[it, k] for k in range(GRP)])

    def gathered(it, value):
        final[it] = value
        for k in range(1, NAR):
            send(
                final.at[it],
                ag_buf.at[it, pl.ds(n * 8, 8)],
                ag_send.at[it, k],
                ag_recv.at[it, k],
                (g, lax.rem(n + k, NAR)),
            )
        ag_buf[it, pl.ds(n * 8, 8)] = value
        for k in range(1, NAR):
            owner = lax.rem(n + NAR - k, NAR)
            arrived(ag_buf.at[it, pl.ds(owner * 8, 8)], ag_recv.at[it, k])

    column_total = reduced(0, joined, log_sum)
    v_one = jnp.log(ref_mass[...]) * LOG2E - column_total
    gathered(0, v_one)
    pick_rows(ag_buf.at[0], rows_a)
    rows_m[...] = jnp.where(alive, jnp.exp2(rows_m[...] + rows_a[...]), 0.0)
    rows_t[...] = rows_m[...]

    def row_sums(b):
        total = None
        for t in range(TOPC):
            e = b * TOPC + t
            p = tiles[e] * rows_t[pl.ds(e, 1)]
            total = p if total is None else total + p
        return jnp.broadcast_to(jnp.sum(total, axis=1, keepdims=True), wide)

    def scale_rows(b, carry):
        r_col[b] = a_col[b] / row_sums(b)
        return carry

    def run_output(b, carry):
        u = (u_col[b] + jnp.log(r_col[b]) * LOG2E) * (0.5 * LN2)
        out_run[pl.ds(b, 1)] = jnp.sum(jnp.where(eye, u, 0.0), axis=0, keepdims=True)
        return carry

    def columns(b, carry):
        alpha = r_col[b]
        for t in range(TOPC):
            e = b * TOPC + t
            rows_a[pl.ds(e, 1)] = jnp.sum(tiles[e] * alpha, axis=0, keepdims=True)
        return carry

    lax.fori_loop(0, RB, scale_rows, 0, unroll=4)
    lax.fori_loop(0, RB, columns, 0, unroll=4)
    second = reduced(1, spread(rows_a[...] * rows_m[...]), plain_sum)
    gathered(1, ref_mass[...] / second)
    pick_rows(ag_buf.at[1], rows_a)
    rows_t[...] = rows_m[...] * rows_a[...]
    lax.fori_loop(0, RB, scale_rows, 0, unroll=4)
    lax.fori_loop(0, RB, columns, 0, unroll=4)
    third = reduced(
        2,
        spread(rows_a[...] * rows_m[...]),
        plain_sum,
        lambda: lax.fori_loop(0, RB, run_output, 0, unroll=2),
    )
    out_ref[...] = (v_one + jnp.log(ref_mass[...] / third) * LOG2E) * (0.5 * LN2)

    for copy in sent:
        copy.wait_send()


def write_out(run_in, ref_in, run_out, ref_out):
    run_out[...] = run_in[...]
    ref_out[...] = ref_in[...]


def shards(run_desc, ref_desc, candidates, live_slots, run_mass, ref_mass, ref_start):
    vmem = pl.BlockSpec(memory_space=pltpu.VMEM)
    hbm = pl.BlockSpec(memory_space=pl.ANY)
    dma = pltpu.SemaphoreType.DMA
    run_potential, ref_potential = pl.pallas_call(
        kernel,
        out_shape=(
            jax.ShapeDtypeStruct((RB, BLK), F32),
            jax.ShapeDtypeStruct((8, BLK), F32),
        ),
        in_specs=[hbm] * 7,
        out_specs=(vmem, vmem),
        scratch_shapes=[
            pltpu.SMEM((TOPC, RB), jnp.int32),
            pltpu.SMEM((RB,), jnp.int32),
            pltpu.VMEM((RB, BLK), F32),
            pltpu.VMEM((8, BLK), F32),
            pltpu.VMEM((8, BLK), F32),
            pltpu.VMEM((REFB, D, BLK), BF16),
            pltpu.VMEM((8, BLK, D), BF16),
            pltpu.VMEM((RB, BLK, D), BF16),
            pltpu.VMEM((ENT, BLK, BLK), F32),
            [pltpu.VMEM((TOPC, BLK, BLK), F32)] * 4,
            [pltpu.VMEM((BLK, BLK), F32)] * 4,
            [pltpu.VMEM((BLK, BLK), F32)] * 4,
            pltpu.VMEM((REFB, BLK), F32),
            pltpu.VMEM((ENT, BLK), F32),
            pltpu.VMEM((ENT, BLK), F32),
            pltpu.VMEM((ENT, BLK), F32),
            pltpu.VMEM((ENT, BLK), F32),
            pltpu.VMEM((ENT, BLK), F32),
            pltpu.VMEM((BLK, ENT), BF16),
            pltpu.VMEM((RB, BLK, BLK), F32),
            pltpu.VMEM((RB, BLK, BLK), F32),
            pltpu.VMEM((RB, BLK, BLK), F32),
            pltpu.VMEM((RB, BLK, BLK), F32),
            pltpu.VMEM((3, REFB, BLK), F32),
            pltpu.VMEM((REFB, BLK), F32),
            pltpu.VMEM((3, NAR, 8, BLK), F32),
            pltpu.VMEM((3, 8, BLK), F32),
            pltpu.VMEM((3, GRP, 8, BLK), F32),
            pltpu.VMEM((2, 8, BLK), F32),
            pltpu.VMEM((2, REFB, BLK), F32),
            pltpu.SemaphoreType.REGULAR,
            dma((7,)),
            dma((1,)),
            dma((32,)),
            dma((30,)),
            dma((31,)),
            dma((31,)),
            dma((NAR,)),
            dma((NAR,)),
            dma((3, NAR)),
            dma((3, NAR)),
            dma((3, GRP)),
            dma((3, GRP)),
            dma((2, NAR)),
            dma((2, NAR)),
        ],
        compiler_params=pltpu.CompilerParams(
            collective_id=0, has_side_effects=True, vmem_limit_bytes=56 * 1024 * 1024
        ),
        name="sinkhorn",
    )(
        candidates.T,
        live_slots,
        run_desc.reshape(RB, BLK, D),
        ref_desc.reshape(8, BLK, D),
        run_mass.reshape(RB, BLK),
        ref_mass.reshape(8, BLK),
        ref_start.reshape(8, BLK),
    )
    run_potential, ref_potential = pl.pallas_call(
        write_out,
        out_shape=(
            jax.ShapeDtypeStruct((RB, BLK), F32),
            jax.ShapeDtypeStruct((8, BLK), F32),
        ),
        in_specs=[vmem, vmem],
        out_specs=(vmem, vmem),
        name="write_out",
    )(run_potential, ref_potential)
    return run_potential.reshape(-1), ref_potential.reshape(-1)


def solution(mesh):
    both = P(("grp", "nar"))
    wide = P(("grp", "nar"), None)
    return jax.shard_map(
        shards,
        mesh=mesh,
        in_specs=(wide, P("nar", None), wide, both, both, P("nar"), P("nar")),
        out_specs=(both, P("nar")),
        check_vma=False,
    )
```

```python
import math

import jax
import jax.numpy as jnp
from jax import lax
from jax.experimental import pallas as pl
from jax.experimental.pallas import tpu as pltpu
from jax.sharding import PartitionSpec as P

BLK = 128
TOPC = 8
RB = 32
ENT = RB * TOPC
D = 256
REFB = 64
NAR = 8
GRP = 16
LOG2E = math.log2(math.e)
LN2 = math.log(2.0)
FLOOR = -1e30
MESH = pl.DeviceIdType.MESH
F32 = jnp.float32
BF16 = jnp.bfloat16


def kernel(
    cand_in,
    live_in,
    run_hbm,
    ref_hbm,
    run_mass_in,
    ref_mass_in,
    start_in,
    out_run,
    out_ref,
    cand,
    live,
    run_mass,
    ref_mass,
    start,
    ref_all,
    own_v,
    run_v,
    tiles,
    raw,
    tops,
    us,
    v_all,
    rows_a,
    rows_m,
    rows_t,
    rows_live,
    onehot_t,
    onehot,
    a_col,
    loga_col,
    r_col,
    u_col,
    dense,
    peak,
    rs_buf,
    part,
    ar_buf,
    final,
    ag_buf,
    here_sem,
    local_sem,
    own_send,
    gather_send,
    gather_recv,
    pair_send,
    pair_recv,
    start_send,
    start_recv,
    rs_send,
    rs_recv,
    ar_send,
    ar_recv,
    ag_send,
    ag_recv,
):
    g = lax.axis_index("grp")
    n = lax.axis_index("nar")
    z, x = lax.div(g, 4), lax.rem(g, 4)
    y, c = lax.div(n, 2), lax.rem(n, 2)

    barrier = pltpu.get_barrier_semaphore()
    partner = (g, y * 2 + 1 - c)
    y_next = (g, lax.rem(y + 1, 4) * 2 + c)
    y_prev = (g, lax.rem(y + 3, 4) * 2 + c)
    x_next = (z * 4 + lax.rem(x + 1, 4), n)
    x_prev = (z * 4 + lax.rem(x + 3, 4), n)
    z_next = (lax.rem(z + 1, 4) * 4 + x, n)
    z_prev = (lax.rem(z + 3, 4) * 4 + x, n)
    y_over = (g, lax.rem(y + 2, 4) * 2 + c)
    x_over = (z * 4 + lax.rem(x + 2, 4), n)
    z_over = (lax.rem(z + 2, 4) * 4 + x, n)
    rings = (y_next, y_prev, y_over, x_next, x_prev, x_over, z_next, z_prev, z_over)
    for to in (*rings, partner):
        pl.semaphore_signal(barrier, inc=1, device_id=to, device_id_type=MESH)

    own_copy = pltpu.make_async_copy(ref_hbm, own_v, local_sem.at[0])
    own_copy.start()
    small = [
        pltpu.make_async_copy(src, dst, local_sem.at[2 + k])
        for k, (src, dst) in enumerate(
            (
                (cand_in, cand),
                (live_in, live),
                (start_in, start),
                (run_mass_in, run_mass),
                (ref_mass_in, ref_mass),
            )
        )
    ]
    for copy in small:
        copy.start()
    run_copy = pltpu.make_async_copy(run_hbm, run_v, local_sem.at[1])
    run_copy.start()

    for copy in small:
        copy.wait()
    own_copy.wait()
    for k in range(8):
        ref_all[n * 8 + k] = own_v[k].T
    lane64 = lax.broadcasted_iota(jnp.int32, (1, BLK), 1)

    def table_step(b, carry):
        for t in range(TOPC):
            e = b * TOPC + t
            onehot_t[pl.ds(e, 1)] = jnp.where(lane64 == cand[t, b], 1.0, 0.0).astype(F32)
            rows_live[pl.ds(e, 1)] = jnp.where(
                jnp.full((1, BLK), t, jnp.int32) < live[b], 1.0, 0.0
            ).astype(F32)
        return carry

    lax.fori_loop(0, RB, table_step, 0, unroll=2)

    pl.semaphore_wait(barrier, 10)
    for to in (z_next, z_prev, z_over, partner):
        pl.semaphore_signal(here_sem, inc=1, device_id=to, device_id_type=MESH)

    s_prev = y_prev[1]
    s_next = y_next[1]
    s_far = lax.rem(y + 2, 4) * 2 + c

    sent = []

    def send(src, dst, send_sem, recv_sem, to):
        copy = pltpu.make_async_remote_copy(
            src_ref=src,
            dst_ref=dst,
            send_sem=send_sem,
            recv_sem=recv_sem,
            device_id=to,
            device_id_type=MESH,
        )
        copy.start()
        sent.append(copy)

    def drain(keep):
        while len(sent) > keep:
            sent.pop(0).wait_send()

    def arrived(dst, recv_sem):
        pltpu.make_async_remote_copy(
            src_ref=dst,
            dst_ref=dst,
            send_sem=own_send.at[0],
            recv_sem=recv_sem,
            device_id=partner,
            device_id_type=MESH,
        ).wait_recv()

    counter = [0]

    def region(block, half):
        if half is None:
            return ref_all.at[block]
        return ref_all.at[block, pl.ds(half * 128, 128)]

    def gsend(block, half, ident, to, src=None):
        dst = region(block, half)
        k = counter[0]
        counter[0] += 1
        send(dst if src is None else src, dst, gather_send.at[k], gather_recv.at[ident], to)

    def to_partner(block, half, ident):
        dst = region(block, half)
        send(dst, dst, pair_send.at[ident], pair_recv.at[ident], partner)

    own_a, own_b = n * 8 + x, n * 8 + 4 + z
    gsend(own_a, None, 0, y_next, ref_all.at[own_a])
    gsend(own_a, None, 1, y_prev, ref_all.at[own_a])
    gsend(own_b, None, 2, y_next, ref_all.at[own_b])
    gsend(own_b, None, 3, y_prev, ref_all.at[own_b])
    gsend(own_a, None, 4, y_over)
    gsend(own_b, None, 5, y_over)
    own_part = ref_all.at[pl.ds(n * 8, 8)]
    send(own_part, own_part, pair_send.at[30], pair_recv.at[30], partner)
    v_all[pl.ds(n * 8, 8)] = start[...]

    eye = lax.broadcasted_iota(jnp.int32, (BLK, BLK), 0) == lax.broadcasted_iota(
        jnp.int32, (BLK, BLK), 1
    )
    wide = (BLK, BLK)

    def column(row):
        spread = jnp.where(eye, jnp.broadcast_to(row, wide), 0.0)
        return jnp.broadcast_to(jnp.sum(spread, axis=1, keepdims=True), wide)

    def mass_step(b, carry):
        row = run_mass[pl.ds(b, 1)]
        a_col[b] = column(row)
        loga_col[b] = column(jnp.log(row) * LOG2E)
        return carry

    lax.fori_loop(0, RB, mass_step, 0)
    onehot[...] = onehot_t[...].T.astype(BF16)

    pl.semaphore_wait(here_sem, 4)
    for k in range(1, NAR):
        send(
            start,
            v_all.at[pl.ds(n * 8, 8)],
            start_send.at[k],
            start_recv.at[k],
            (g, lax.rem(n + k, NAR)),
        )

    a_prev, a_next, a_far = s_prev * 8 + x, s_next * 8 + x, s_far * 8 + x
    b_prev, b_next, b_far = s_prev * 8 + 4 + z, s_next * 8 + 4 + z, s_far * 8 + 4 + z

    def y_piece(block, ident, j, along_x):
        arrived(region(block, None), gather_recv.at[ident])
        base = 6 if along_x else 18
        up, down = (x_next, x_prev) if along_x else (z_next, z_prev)
        gsend(block, None, base + j, up)
        gsend(block, None, base + 3 + j, down)
        gsend(block, None, base + 6 + j, x_over if along_x else z_over)
        to_partner(block, None, ident)

    y_piece(a_prev, 0, 0, True)
    y_piece(b_next, 3, 1, False)
    y_piece(a_next, 1, 1, True)
    y_piece(b_prev, 2, 0, False)
    y_piece(a_far, 4, 2, True)
    y_piece(b_far, 5, 2, False)

    shard = (s_prev, s_next, s_far)
    x_up, x_down, x_far = lax.rem(x + 3, 4), lax.rem(x + 1, 4), lax.rem(x + 2, 4)
    z_up, z_down, z_far = lax.rem(z + 3, 4), lax.rem(z + 1, 4), lax.rem(z + 2, 4)

    def ring_piece(j, along_x):
        base = 6 if along_x else 18
        off = 0 if along_x else 4
        from_prev = shard[j] * 8 + off + (x_up if along_x else z_up)
        from_next = shard[j] * 8 + off + (x_down if along_x else z_down)
        up, down = (x_next, x_prev) if along_x else (z_next, z_prev)
        arrived(region(from_prev, None), gather_recv.at[base + j])
        to_partner(from_prev, None, base + j)
        arrived(region(from_next, None), gather_recv.at[base + 3 + j])
        to_partner(from_next, None, base + 3 + j)

    def far_piece(j, along_x):
        base = 6 if along_x else 18
        off = 0 if along_x else 4
        block = shard[j] * 8 + off + (x_far if along_x else z_far)
        arrived(region(block, None), gather_recv.at[base + 6 + j])
        to_partner(block, None, base + 6 + j)

    ring_piece(0, True)
    ring_piece(1, False)
    ring_piece(1, True)
    ring_piece(0, False)
    ring_piece(2, True)
    ring_piece(2, False)

    far_piece(0, True)
    far_piece(1, False)
    far_piece(1, True)
    far_piece(0, False)
    far_piece(2, True)
    far_piece(2, False)

    for k in range(1, NAR):
        owner = lax.rem(n + NAR - k, NAR)
        arrived(v_all.at[pl.ds(owner * 8, 8)], start_recv.at[k])

    def pick_rows(table, to):
        def step(b, carry):
            for t in range(TOPC):
                to[pl.ds(b * TOPC + t, 1)] = table[pl.ds(cand[t, b], 1)]
            return carry

        lax.fori_loop(0, RB, step, 0, unroll=4)

    pick_rows(v_all, rows_a)
    alive = rows_live[...] > 0.5
    rows_a[...] = jnp.where(alive, rows_a[...] * (2.0 * LOG2E), FLOOR)

    other = partner[1]
    arrived(ref_all.at[pl.ds(other * 8, 8)], pair_recv.at[30])
    o_shard = tuple(s + 1 - 2 * c for s in shard)
    pieces = []
    pieces += [(o_shard[0] * 8 + x, None, 0), (o_shard[1] * 8 + x, None, 1)]
    pieces += [(o_shard[0] * 8 + 4 + z, None, 2), (o_shard[1] * 8 + 4 + z, None, 3)]
    pieces += [(o_shard[2] * 8 + x, None, 4), (o_shard[2] * 8 + 4 + z, None, 5)]
    for j in range(3):
        for base, off, up, down, far in (
            (6, 0, x_up, x_down, x_far),
            (18, 4, z_up, z_down, z_far),
        ):
            pieces.append((o_shard[j] * 8 + off + up, None, base + j))
            pieces.append((o_shard[j] * 8 + off + down, None, base + 3 + j))
            pieces.append((o_shard[j] * 8 + off + far, None, base + 6 + j))
    for block, half, ident in pieces:
        arrived(region(block, half), pair_recv.at[ident])
    run_copy.wait()

    def cost_part(b, slot, h, top):
        both = jnp.concatenate([ref_all[cand[2 * h, b]], ref_all[cand[2 * h + 1, b]]], axis=1)
        prod = lax.dot_general(
            run_v[b], both, (((1,), (0,)), ((), ())), preferred_element_type=F32
        ) * (LOG2E / 8.0)
        for q in range(2):
            s = prod[:, q * BLK : (q + 1) * BLK]
            raw[slot][2 * h + q] = s
            s = s + rows_a[pl.ds(b * TOPC + 2 * h + q, 1)]
            top = s if top is None else jnp.maximum(top, s)
        return top

    def cost_end(slot, top):
        tops[slot][...] = jnp.broadcast_to(jnp.max(top, axis=1, keepdims=True), wide)

    def row_part(b, slot, h, total):
        for t in (2 * h, 2 * h + 1):
            p = jnp.exp2(raw[slot][t] + rows_a[pl.ds(b * TOPC + t, 1)] - tops[slot][...])
            total = p if total is None else total + p
        return total

    def row_end(b, slot, total):
        total = jnp.broadcast_to(jnp.sum(total, axis=1, keepdims=True), wide)
        u = loga_col[b] - (tops[slot][...] + jnp.log(total) * LOG2E)
        u_col[b] = u
        us[slot][...] = u

    def column_part(b, slot, h):
        for t in (2 * h, 2 * h + 1):
            e = b * TOPC + t
            s = raw[slot][t] + us[slot][...]
            m = jnp.max(s, axis=0, keepdims=True)
            p = jnp.exp2(s - m)
            tiles[e] = p
            rows_m[pl.ds(e, 1)] = m
            rows_t[pl.ds(e, 1)] = jnp.sum(p, axis=0, keepdims=True)

    def stage(b, at, cost=True, row=True, col=True):
        top = total = None
        for h in range(TOPC // 2):
            if col:
                column_part(b - 2, (at + 2) % 4, h)
            if row:
                total = row_part(b - 1, (at + 3) % 4, h, total)
            if cost:
                top = cost_part(b, at, h, top)
        if row:
            row_end(b - 1, (at + 3) % 4, total)
        if cost:
            cost_end(at, top)

    stage(0, 0, row=False, col=False)
    stage(1, 1, col=False)

    def first_step(k, carry):
        for q in range(4):
            stage(2 + 4 * k + q, (2 + q) % 4)
        return carry

    lax.fori_loop(0, 28 // 4, first_step, 0)
    stage(30, 2)
    stage(31, 3)
    stage(32, 0, cost=False)
    stage(33, 1, cost=False, row=False)
    alive = rows_live[...] > 0.5
    rows_m[...] = jnp.where(alive, rows_m[...], FLOOR)
    block_id = lax.broadcasted_iota(jnp.int32, (REFB, BLK), 0)

    def peak_step(b, top):
        for t in range(TOPC):
            e = b * TOPC + t
            top = jnp.maximum(
                top, jnp.where(block_id == cand[t, b], rows_m[pl.ds(e, 1)], FLOOR)
            )
        return top

    top = lax.fori_loop(0, RB, peak_step, jnp.full((REFB, BLK), FLOOR, F32), unroll=2)
    peak[...] = top
    pick_rows(peak, rows_a)

    def spread(rows):
        hi = rows.astype(BF16)
        rest = rows - hi.astype(F32)
        mid = rest.astype(BF16)
        low = (rest - mid.astype(F32)).astype(BF16)
        total = None
        for piece in (hi, mid, low):
            d = lax.dot_general(
                onehot[0:REFB], piece, (((1,), (0,)), ((), ())), preferred_element_type=F32
            )
            total = d if total is None else total + d
        return total

    scaled = jnp.where(alive, rows_t[...] * jnp.exp2(rows_m[...] - rows_a[...]), 0.0)
    total = spread(scaled)
    joined = jnp.where(total > 0.0, peak[...] + jnp.log(total) * LOG2E, FLOOR)

    def log_sum(parts):
        top = parts[0]
        for p in parts[1:]:
            top = jnp.maximum(top, p)
        total = None
        for p in parts:
            e = jnp.exp2(p - top)
            total = e if total is None else total + e
        return top + jnp.log(total) * LOG2E

    def plain_sum(parts):
        total = parts[0]
        for p in parts[1:]:
            total = total + p
        return total

    def reduced(it, value, join, meanwhile=None):
        dense[it] = value
        for k in range(1, NAR):
            to = lax.rem(n + k, NAR)
            send(
                dense.at[it, pl.ds(to * 8, 8)],
                rs_buf.at[it, n],
                rs_send.at[it, k],
                rs_recv.at[it, k],
                (g, to),
            )
        rs_buf[it, n] = dense[it, pl.ds(n * 8, 8)]
        drain(NAR - 1)
        if meanwhile is not None:
            meanwhile()
        for k in range(1, NAR):
            arrived(rs_buf.at[it, lax.rem(n + NAR - k, NAR)], rs_recv.at[it, k])
        mine = join([rs_buf[it, k] for k in range(NAR)])
        part[it] = mine
        for k in range(1, GRP):
            send(
                part.at[it],
                ar_buf.at[it, g],
                ar_send.at[it, k],
                ar_recv.at[it, k],
                (lax.rem(g + k, GRP), n),
            )
        ar_buf[it, g] = mine
        drain(GRP - 1)
        for k in range(1, GRP):
            arrived(ar_buf.at[it, lax.rem(g + GRP - k, GRP)], ar_recv.at[it, k])
        return join([ar_buf[it, k] for k in range(GRP)])

    def gathered(it, value):
        final[it] = value
        for k in range(1, NAR):
            send(
                final.at[it],
                ag_buf.at[it, pl.ds(n * 8, 8)],
                ag_send.at[it, k],
                ag_recv.at[it, k],
                (g, lax.rem(n + k, NAR)),
            )
        ag_buf[it, pl.ds(n * 8, 8)] = value
        drain(NAR - 1)
        for k in range(1, NAR):
            owner = lax.rem(n + NAR - k, NAR)
            arrived(ag_buf.at[it, pl.ds(owner * 8, 8)], ag_recv.at[it, k])

    column_total = reduced(0, joined, log_sum)
    v_one = jnp.log(ref_mass[...]) * LOG2E - column_total
    gathered(0, v_one)
    pick_rows(ag_buf.at[0], rows_a)
    rows_m[...] = jnp.where(alive, jnp.exp2(rows_m[...] + rows_a[...]), 0.0)
    rows_t[...] = rows_m[...]

    def row_sums(b):
        total = None
        for t in range(TOPC):
            e = b * TOPC + t
            p = tiles[e] * rows_t[pl.ds(e, 1)]
            total = p if total is None else total + p
        return jnp.broadcast_to(jnp.sum(total, axis=1, keepdims=True), wide)

    def scale_rows(b, slot):
        alpha = a_col[b] / row_sums(b)
        r_col[b] = alpha
        tops[slot][...] = alpha

    def run_output(b, carry):
        u = (u_col[b] + jnp.log(r_col[b]) * LOG2E) * (0.5 * LN2)
        out_run[pl.ds(b, 1)] = jnp.sum(jnp.where(eye, u, 0.0), axis=0, keepdims=True)
        return carry

    def columns(b, slot):
        alpha = tops[slot][...]
        for t in range(TOPC):
            e = b * TOPC + t
            rows_a[pl.ds(e, 1)] = jnp.sum(tiles[e] * alpha, axis=0, keepdims=True)

    def both_sides():
        def step(k, carry):
            for q in range(4):
                scale_rows(1 + 4 * k + q, (1 + q) % 4)
                columns(4 * k + q, q)
            return carry

        scale_rows(0, 0)
        lax.fori_loop(0, 7, step, 0)
        for b in range(28, 31):
            scale_rows(b + 1, (b + 1) % 4)
            columns(b, b % 4)
        columns(31, 3)

    both_sides()
    second = reduced(1, spread(rows_a[...] * rows_m[...]), plain_sum)
    gathered(1, ref_mass[...] / second)
    pick_rows(ag_buf.at[1], rows_a)
    rows_t[...] = rows_m[...] * rows_a[...]
    both_sides()
    third = reduced(
        2,
        spread(rows_a[...] * rows_m[...]),
        plain_sum,
        lambda: lax.fori_loop(0, RB, run_output, 0, unroll=2),
    )
    out_ref[...] = (v_one + jnp.log(ref_mass[...] / third) * LOG2E) * (0.5 * LN2)

    drain(0)


def write_out(run_in, ref_in, run_out, ref_out):
    run_out[...] = run_in[...]
    ref_out[...] = ref_in[...]


def shards(run_desc, ref_desc, candidates, live_slots, run_mass, ref_mass, ref_start):
    vmem = pl.BlockSpec(memory_space=pltpu.VMEM)
    hbm = pl.BlockSpec(memory_space=pl.ANY)
    dma = pltpu.SemaphoreType.DMA
    run_potential, ref_potential = pl.pallas_call(
        kernel,
        out_shape=(
            jax.ShapeDtypeStruct((RB, BLK), F32),
            jax.ShapeDtypeStruct((8, BLK), F32),
        ),
        in_specs=[hbm] * 7,
        out_specs=(vmem, vmem),
        scratch_shapes=[
            pltpu.SMEM((TOPC, RB), jnp.int32),
            pltpu.SMEM((RB,), jnp.int32),
            pltpu.VMEM((RB, BLK), F32),
            pltpu.VMEM((8, BLK), F32),
            pltpu.VMEM((8, BLK), F32),
            pltpu.VMEM((REFB, D, BLK), BF16),
            pltpu.VMEM((8, BLK, D), BF16),
            pltpu.VMEM((RB, BLK, D), BF16),
            pltpu.VMEM((ENT, BLK, BLK), F32),
            [pltpu.VMEM((TOPC, BLK, BLK), F32)] * 4,
            [pltpu.VMEM((BLK, BLK), F32)] * 4,
            [pltpu.VMEM((BLK, BLK), F32)] * 4,
            pltpu.VMEM((REFB, BLK), F32),
            pltpu.VMEM((ENT, BLK), F32),
            pltpu.VMEM((ENT, BLK), F32),
            pltpu.VMEM((ENT, BLK), F32),
            pltpu.VMEM((ENT, BLK), F32),
            pltpu.VMEM((ENT, BLK), F32),
            pltpu.VMEM((BLK, ENT), BF16),
            pltpu.VMEM((RB, BLK, BLK), F32),
            pltpu.VMEM((RB, BLK, BLK), F32),
            pltpu.VMEM((RB, BLK, BLK), F32),
            pltpu.VMEM((RB, BLK, BLK), F32),
            pltpu.VMEM((3, REFB, BLK), F32),
            pltpu.VMEM((REFB, BLK), F32),
            pltpu.VMEM((3, NAR, 8, BLK), F32),
            pltpu.VMEM((3, 8, BLK), F32),
            pltpu.VMEM((3, GRP, 8, BLK), F32),
            pltpu.VMEM((2, 8, BLK), F32),
            pltpu.VMEM((2, REFB, BLK), F32),
            pltpu.SemaphoreType.REGULAR,
            dma((7,)),
            dma((1,)),
            dma((32,)),
            dma((30,)),
            dma((31,)),
            dma((31,)),
            dma((NAR,)),
            dma((NAR,)),
            dma((3, NAR)),
            dma((3, NAR)),
            dma((3, GRP)),
            dma((3, GRP)),
            dma((2, NAR)),
            dma((2, NAR)),
        ],
        compiler_params=pltpu.CompilerParams(
            collective_id=0, has_side_effects=True, vmem_limit_bytes=56 * 1024 * 1024
        ),
        name="sinkhorn",
    )(
        candidates.T,
        live_slots,
        run_desc.reshape(RB, BLK, D),
        ref_desc.reshape(8, BLK, D),
        run_mass.reshape(RB, BLK),
        ref_mass.reshape(8, BLK),
        ref_start.reshape(8, BLK),
    )
    run_potential, ref_potential = pl.pallas_call(
        write_out,
        out_shape=(
            jax.ShapeDtypeStruct((RB, BLK), F32),
            jax.ShapeDtypeStruct((8, BLK), F32),
        ),
        in_specs=[vmem, vmem],
        out_specs=(vmem, vmem),
        name="write_out",
    )(run_potential, ref_potential)
    return run_potential.reshape(-1), ref_potential.reshape(-1)


def solution(mesh):
    both = P(("grp", "nar"))
    wide = P(("grp", "nar"), None)
    return jax.shard_map(
        shards,
        mesh=mesh,
        in_specs=(wide, P("nar", None), wide, both, both, P("nar"), P("nar")),
        out_specs=(both, P("nar")),
        check_vma=False,
    )
```

```python
import math

import jax
import jax.numpy as jnp
from jax import lax
from jax.experimental import pallas as pl
from jax.experimental.pallas import tpu as pltpu
from jax.sharding import PartitionSpec as P

BLK = 128
TOPC = 8
RB = 32
ENT = RB * TOPC
D = 256
REFB = 64
NAR = 8
GRP = 16
LOG2E = math.log2(math.e)
LN2 = math.log(2.0)
FLOOR = -1e30
MESH = pl.DeviceIdType.MESH
F32 = jnp.float32
BF16 = jnp.bfloat16


def kernel(
    cand_in,
    live_in,
    run_hbm,
    ref_hbm,
    run_mass_in,
    ref_mass_in,
    start_in,
    out_run,
    out_ref,
    cand,
    live,
    run_mass,
    ref_mass,
    start,
    ref_all,
    own_v,
    run_v,
    tiles,
    raw,
    tops,
    us,
    v_all,
    rows_a,
    rows_m,
    rows_t,
    rows_live,
    onehot_t,
    onehot,
    a_col,
    loga_col,
    r_col,
    u_col,
    dense,
    peak,
    rs_buf,
    part,
    ar_buf,
    final,
    ag_buf,
    here_sem,
    local_sem,
    own_send,
    gather_send,
    gather_recv,
    pair_send,
    pair_recv,
    start_send,
    start_recv,
    rs_send,
    rs_recv,
    ar_send,
    ar_recv,
    ag_send,
    ag_recv,
):
    g = lax.axis_index("grp")
    n = lax.axis_index("nar")
    z, x = lax.div(g, 4), lax.rem(g, 4)
    y, c = lax.div(n, 2), lax.rem(n, 2)

    barrier = pltpu.get_barrier_semaphore()
    partner = (g, y * 2 + 1 - c)
    y_next = (g, lax.rem(y + 1, 4) * 2 + c)
    y_prev = (g, lax.rem(y + 3, 4) * 2 + c)
    x_next = (z * 4 + lax.rem(x + 1, 4), n)
    x_prev = (z * 4 + lax.rem(x + 3, 4), n)
    z_next = (lax.rem(z + 1, 4) * 4 + x, n)
    z_prev = (lax.rem(z + 3, 4) * 4 + x, n)
    y_over = (g, lax.rem(y + 2, 4) * 2 + c)
    x_over = (z * 4 + lax.rem(x + 2, 4), n)
    z_over = (lax.rem(z + 2, 4) * 4 + x, n)
    rings = (y_next, y_prev, y_over, x_next, x_prev, x_over, z_next, z_prev, z_over)
    for to in (*rings, partner):
        pl.semaphore_signal(barrier, inc=1, device_id=to, device_id_type=MESH)

    own_copy = pltpu.make_async_copy(ref_hbm, own_v, local_sem.at[0])
    own_copy.start()
    small = [
        pltpu.make_async_copy(src, dst, local_sem.at[2 + k])
        for k, (src, dst) in enumerate(
            (
                (cand_in, cand),
                (live_in, live),
                (start_in, start),
                (run_mass_in, run_mass),
                (ref_mass_in, ref_mass),
            )
        )
    ]
    for copy in small:
        copy.start()
    run_copy = pltpu.make_async_copy(run_hbm, run_v, local_sem.at[1])
    run_copy.start()

    for copy in small:
        copy.wait()
    own_copy.wait()
    for k in range(8):
        ref_all[n * 8 + k] = own_v[k].T
    lane64 = lax.broadcasted_iota(jnp.int32, (1, BLK), 1)

    def table_step(b, carry):
        for t in range(TOPC):
            e = b * TOPC + t
            onehot_t[pl.ds(e, 1)] = jnp.where(lane64 == cand[t, b], 1.0, 0.0).astype(F32)
            rows_live[pl.ds(e, 1)] = jnp.where(
                jnp.full((1, BLK), t, jnp.int32) < live[b], 1.0, 0.0
            ).astype(F32)
        return carry

    lax.fori_loop(0, RB, table_step, 0, unroll=2)

    pl.semaphore_wait(barrier, 10)
    for to in (z_next, z_prev, z_over, partner):
        pl.semaphore_signal(here_sem, inc=1, device_id=to, device_id_type=MESH)

    s_prev = y_prev[1]
    s_next = y_next[1]
    s_far = lax.rem(y + 2, 4) * 2 + c

    sent = []

    def send(src, dst, send_sem, recv_sem, to):
        copy = pltpu.make_async_remote_copy(
            src_ref=src,
            dst_ref=dst,
            send_sem=send_sem,
            recv_sem=recv_sem,
            device_id=to,
            device_id_type=MESH,
        )
        copy.start()
        sent.append(copy)

    def drain(keep):
        while len(sent) > keep:
            sent.pop(0).wait_send()

    def arrived(dst, recv_sem):
        pltpu.make_async_remote_copy(
            src_ref=dst,
            dst_ref=dst,
            send_sem=own_send.at[0],
            recv_sem=recv_sem,
            device_id=partner,
            device_id_type=MESH,
        ).wait_recv()

    counter = [0]

    def region(block, half):
        if half is None:
            return ref_all.at[block]
        return ref_all.at[block, pl.ds(half * 128, 128)]

    def gsend(block, half, ident, to, src=None):
        dst = region(block, half)
        k = counter[0]
        counter[0] += 1
        send(dst if src is None else src, dst, gather_send.at[k], gather_recv.at[ident], to)

    def to_partner(block, half, ident):
        dst = region(block, half)
        send(dst, dst, pair_send.at[ident], pair_recv.at[ident], partner)

    own_a, own_b = n * 8 + x, n * 8 + 4 + z
    gsend(own_a, None, 0, y_next, ref_all.at[own_a])
    gsend(own_a, None, 1, y_prev, ref_all.at[own_a])
    gsend(own_b, None, 2, y_next, ref_all.at[own_b])
    gsend(own_b, None, 3, y_prev, ref_all.at[own_b])
    gsend(own_a, None, 4, y_over)
    gsend(own_b, None, 5, y_over)
    own_part = ref_all.at[pl.ds(n * 8, 8)]
    send(own_part, own_part, pair_send.at[30], pair_recv.at[30], partner)
    v_all[pl.ds(n * 8, 8)] = start[...]

    eye = lax.broadcasted_iota(jnp.int32, (BLK, BLK), 0) == lax.broadcasted_iota(
        jnp.int32, (BLK, BLK), 1
    )
    wide = (BLK, BLK)

    def column(row):
        spread = jnp.where(eye, jnp.broadcast_to(row, wide), 0.0)
        return jnp.broadcast_to(jnp.sum(spread, axis=1, keepdims=True), wide)

    def mass_step(b, carry):
        row = run_mass[pl.ds(b, 1)]
        a_col[b] = column(row)
        loga_col[b] = column(jnp.log(row) * LOG2E)
        return carry

    lax.fori_loop(0, RB, mass_step, 0)
    onehot[...] = onehot_t[...].T.astype(BF16)

    pl.semaphore_wait(here_sem, 4)
    for k in range(1, NAR):
        send(
            start,
            v_all.at[pl.ds(n * 8, 8)],
            start_send.at[k],
            start_recv.at[k],
            (g, lax.rem(n + k, NAR)),
        )

    a_prev, a_next, a_far = s_prev * 8 + x, s_next * 8 + x, s_far * 8 + x
    b_prev, b_next, b_far = s_prev * 8 + 4 + z, s_next * 8 + 4 + z, s_far * 8 + 4 + z

    def y_piece(block, ident, j, along_x):
        arrived(region(block, None), gather_recv.at[ident])
        base = 6 if along_x else 18
        up, down = (x_next, x_prev) if along_x else (z_next, z_prev)
        gsend(block, None, base + j, up)
        gsend(block, None, base + 3 + j, down)
        gsend(block, None, base + 6 + j, x_over if along_x else z_over)
        to_partner(block, None, ident)

    y_piece(a_prev, 0, 0, True)
    y_piece(b_next, 3, 1, False)
    y_piece(a_next, 1, 1, True)
    y_piece(b_prev, 2, 0, False)
    y_piece(a_far, 4, 2, True)
    y_piece(b_far, 5, 2, False)

    shard = (s_prev, s_next, s_far)
    x_up, x_down, x_far = lax.rem(x + 3, 4), lax.rem(x + 1, 4), lax.rem(x + 2, 4)
    z_up, z_down, z_far = lax.rem(z + 3, 4), lax.rem(z + 1, 4), lax.rem(z + 2, 4)

    def ring_piece(j, along_x):
        base = 6 if along_x else 18
        off = 0 if along_x else 4
        from_prev = shard[j] * 8 + off + (x_up if along_x else z_up)
        from_next = shard[j] * 8 + off + (x_down if along_x else z_down)
        up, down = (x_next, x_prev) if along_x else (z_next, z_prev)
        arrived(region(from_prev, None), gather_recv.at[base + j])
        to_partner(from_prev, None, base + j)
        arrived(region(from_next, None), gather_recv.at[base + 3 + j])
        to_partner(from_next, None, base + 3 + j)

    def far_piece(j, along_x):
        base = 6 if along_x else 18
        off = 0 if along_x else 4
        block = shard[j] * 8 + off + (x_far if along_x else z_far)
        arrived(region(block, None), gather_recv.at[base + 6 + j])
        to_partner(block, None, base + 6 + j)

    ring_piece(0, True)
    ring_piece(1, False)
    ring_piece(1, True)
    ring_piece(0, False)
    ring_piece(2, True)
    ring_piece(2, False)

    far_piece(0, True)
    far_piece(1, False)
    far_piece(1, True)
    far_piece(0, False)
    far_piece(2, True)
    far_piece(2, False)

    for k in range(1, NAR):
        owner = lax.rem(n + NAR - k, NAR)
        arrived(v_all.at[pl.ds(owner * 8, 8)], start_recv.at[k])

    def pick_rows(table, to):
        def step(b, carry):
            for t in range(TOPC):
                to[pl.ds(b * TOPC + t, 1)] = table[pl.ds(cand[t, b], 1)]
            return carry

        lax.fori_loop(0, RB, step, 0, unroll=4)

    pick_rows(v_all, rows_a)
    alive = rows_live[...] > 0.5
    rows_a[...] = jnp.where(alive, rows_a[...] * (2.0 * LOG2E), FLOOR)

    other = partner[1]
    arrived(ref_all.at[pl.ds(other * 8, 8)], pair_recv.at[30])
    o_shard = tuple(s + 1 - 2 * c for s in shard)
    pieces = []
    pieces += [(o_shard[0] * 8 + x, None, 0), (o_shard[1] * 8 + x, None, 1)]
    pieces += [(o_shard[0] * 8 + 4 + z, None, 2), (o_shard[1] * 8 + 4 + z, None, 3)]
    pieces += [(o_shard[2] * 8 + x, None, 4), (o_shard[2] * 8 + 4 + z, None, 5)]
    for j in range(3):
        for base, off, up, down, far in (
            (6, 0, x_up, x_down, x_far),
            (18, 4, z_up, z_down, z_far),
        ):
            pieces.append((o_shard[j] * 8 + off + up, None, base + j))
            pieces.append((o_shard[j] * 8 + off + down, None, base + 3 + j))
            pieces.append((o_shard[j] * 8 + off + far, None, base + 6 + j))
    for block, half, ident in pieces:
        arrived(region(block, half), pair_recv.at[ident])
    run_copy.wait()

    def cost_part(b, slot, h, top):
        both = jnp.concatenate([ref_all[cand[2 * h, b]], ref_all[cand[2 * h + 1, b]]], axis=1)
        prod = lax.dot_general(
            run_v[b], both, (((1,), (0,)), ((), ())), preferred_element_type=F32
        ) * (LOG2E / 8.0)
        for q in range(2):
            s = prod[:, q * BLK : (q + 1) * BLK]
            raw[slot][2 * h + q] = s
            s = s + rows_a[pl.ds(b * TOPC + 2 * h + q, 1)]
            top = s if top is None else jnp.maximum(top, s)
        return top

    def cost_end(slot, top):
        tops[slot][...] = jnp.broadcast_to(jnp.max(top, axis=1, keepdims=True), wide)

    def row_part(b, slot, h, total):
        for t in (2 * h, 2 * h + 1):
            p = jnp.exp2(raw[slot][t] + rows_a[pl.ds(b * TOPC + t, 1)] - tops[slot][...])
            total = p if total is None else total + p
        return total

    def row_end(b, slot, total):
        total = jnp.broadcast_to(jnp.sum(total, axis=1, keepdims=True), wide)
        u = loga_col[b] - (tops[slot][...] + jnp.log(total) * LOG2E)
        u_col[b] = u
        us[slot][...] = u

    def column_part(b, slot, h):
        for t in (2 * h, 2 * h + 1):
            e = b * TOPC + t
            s = raw[slot][t] + us[slot][...]
            m = jnp.max(s, axis=0, keepdims=True)
            p = jnp.exp2(s - m)
            tiles[e] = p
            rows_m[pl.ds(e, 1)] = m
            rows_t[pl.ds(e, 1)] = jnp.sum(p, axis=0, keepdims=True)

    def stage(b, at, cost=True, row=True, col=True):
        top = total = None
        for h in range(TOPC // 2):
            if col:
                column_part(b - 2, (at + 2) % 4, h)
            if row:
                total = row_part(b - 1, (at + 3) % 4, h, total)
            if cost:
                top = cost_part(b, at, h, top)
        if row:
            row_end(b - 1, (at + 3) % 4, total)
        if cost:
            cost_end(at, top)

    stage(0, 0, row=False, col=False)
    stage(1, 1, col=False)

    def first_step(k, carry):
        for q in range(4):
            stage(2 + 4 * k + q, (2 + q) % 4)
        return carry

    lax.fori_loop(0, 28 // 4, first_step, 0)
    stage(30, 2)
    stage(31, 3)
    stage(32, 0, cost=False)
    stage(33, 1, cost=False, row=False)
    alive = rows_live[...] > 0.5
    rows_m[...] = jnp.where(alive, rows_m[...], FLOOR)
    block_id = lax.broadcasted_iota(jnp.int32, (REFB, BLK), 0)

    def peak_step(b, top):
        for t in range(TOPC):
            e = b * TOPC + t
            top = jnp.maximum(
                top, jnp.where(block_id == cand[t, b], rows_m[pl.ds(e, 1)], FLOOR)
            )
        return top

    top = lax.fori_loop(0, RB, peak_step, jnp.full((REFB, BLK), FLOOR, F32), unroll=2)
    peak[...] = top
    pick_rows(peak, rows_a)

    def spread(rows):
        hi = rows.astype(BF16)
        rest = rows - hi.astype(F32)
        mid = rest.astype(BF16)
        low = (rest - mid.astype(F32)).astype(BF16)
        total = None
        for piece in (hi, mid, low):
            d = lax.dot_general(
                onehot[0:REFB], piece, (((1,), (0,)), ((), ())), preferred_element_type=F32
            )
            total = d if total is None else total + d
        return total

    scaled = jnp.where(alive, rows_t[...] * jnp.exp2(rows_m[...] - rows_a[...]), 0.0)
    total = spread(scaled)
    joined = jnp.where(total > 0.0, peak[...] + jnp.log(total) * LOG2E, FLOOR)

    def log_sum(parts):
        top = parts[0]
        for p in parts[1:]:
            top = jnp.maximum(top, p)
        total = None
        for p in parts:
            e = jnp.exp2(p - top)
            total = e if total is None else total + e
        return top + jnp.log(total) * LOG2E

    def plain_sum(parts):
        total = parts[0]
        for p in parts[1:]:
            total = total + p
        return total

    def reduced(it, value, join, meanwhile=None):
        dense[it] = value
        for k in range(1, NAR):
            to = lax.rem(n + k, NAR)
            send(
                dense.at[it, pl.ds(to * 8, 8)],
                rs_buf.at[it, n],
                rs_send.at[it, k],
                rs_recv.at[it, k],
                (g, to),
            )
        rs_buf[it, n] = dense[it, pl.ds(n * 8, 8)]
        drain(NAR - 1)
        if meanwhile is not None:
            meanwhile()
        for k in range(1, NAR):
            arrived(rs_buf.at[it, lax.rem(n + NAR - k, NAR)], rs_recv.at[it, k])
        mine = join([rs_buf[it, k] for k in range(NAR)])
        part[it] = mine
        for k in (10, 6, 9, 11, 5, 7, 8, 2, 14, 13, 1, 3, 15, 4, 12):
            send(
                part.at[it],
                ar_buf.at[it, g],
                ar_send.at[it, k],
                ar_recv.at[it, k],
                (lax.rem(g + k, GRP), n),
            )
        ar_buf[it, g] = mine
        drain(GRP - 1)
        for k in range(1, GRP):
            arrived(ar_buf.at[it, lax.rem(g + GRP - k, GRP)], ar_recv.at[it, k])
        return join([ar_buf[it, k] for k in range(GRP)])

    def gathered(it, value):
        final[it] = value
        for k in range(1, NAR):
            send(
                final.at[it],
                ag_buf.at[it, pl.ds(n * 8, 8)],
                ag_send.at[it, k],
                ag_recv.at[it, k],
                (g, lax.rem(n + k, NAR)),
            )
        ag_buf[it, pl.ds(n * 8, 8)] = value
        drain(NAR - 1)
        for k in range(1, NAR):
            owner = lax.rem(n + NAR - k, NAR)
            arrived(ag_buf.at[it, pl.ds(owner * 8, 8)], ag_recv.at[it, k])

    column_total = reduced(0, joined, log_sum)
    v_one = jnp.log(ref_mass[...]) * LOG2E - column_total
    gathered(0, v_one)
    pick_rows(ag_buf.at[0], rows_a)
    rows_m[...] = jnp.where(alive, jnp.exp2(rows_m[...] + rows_a[...]), 0.0)
    rows_t[...] = rows_m[...]

    def row_sums(b):
        total = None
        for t in range(TOPC):
            e = b * TOPC + t
            p = tiles[e] * rows_t[pl.ds(e, 1)]
            total = p if total is None else total + p
        return jnp.broadcast_to(jnp.sum(total, axis=1, keepdims=True), wide)

    def scale_rows(b, slot):
        alpha = a_col[b] / row_sums(b)
        r_col[b] = alpha
        tops[slot][...] = alpha

    def run_output(b, carry):
        u = (u_col[b] + jnp.log(r_col[b]) * LOG2E) * (0.5 * LN2)
        out_run[pl.ds(b, 1)] = jnp.sum(jnp.where(eye, u, 0.0), axis=0, keepdims=True)
        return carry

    def columns(b, slot):
        alpha = tops[slot][...]
        for t in range(TOPC):
            e = b * TOPC + t
            rows_a[pl.ds(e, 1)] = jnp.sum(tiles[e] * alpha, axis=0, keepdims=True)

    def both_sides():
        def step(k, carry):
            for q in range(4):
                scale_rows(1 + 4 * k + q, (1 + q) % 4)
                columns(4 * k + q, q)
            return carry

        scale_rows(0, 0)
        lax.fori_loop(0, 7, step, 0)
        for b in range(28, 31):
            scale_rows(b + 1, (b + 1) % 4)
            columns(b, b % 4)
        columns(31, 3)

    both_sides()
    second = reduced(1, spread(rows_a[...] * rows_m[...]), plain_sum)
    gathered(1, ref_mass[...] / second)
    pick_rows(ag_buf.at[1], rows_a)
    rows_t[...] = rows_m[...] * rows_a[...]
    both_sides()
    third = reduced(
        2,
        spread(rows_a[...] * rows_m[...]),
        plain_sum,
        lambda: lax.fori_loop(0, RB, run_output, 0, unroll=2),
    )
    out_ref[...] = (v_one + jnp.log(ref_mass[...] / third) * LOG2E) * (0.5 * LN2)

    drain(0)


def write_out(run_in, ref_in, run_out, ref_out):
    run_out[...] = run_in[...]
    ref_out[...] = ref_in[...]


def shards(run_desc, ref_desc, candidates, live_slots, run_mass, ref_mass, ref_start):
    vmem = pl.BlockSpec(memory_space=pltpu.VMEM)
    hbm = pl.BlockSpec(memory_space=pl.ANY)
    dma = pltpu.SemaphoreType.DMA
    run_potential, ref_potential = pl.pallas_call(
        kernel,
        out_shape=(
            jax.ShapeDtypeStruct((RB, BLK), F32),
            jax.ShapeDtypeStruct((8, BLK), F32),
        ),
        in_specs=[hbm] * 7,
        out_specs=(vmem, vmem),
        scratch_shapes=[
            pltpu.SMEM((TOPC, RB), jnp.int32),
            pltpu.SMEM((RB,), jnp.int32),
            pltpu.VMEM((RB, BLK), F32),
            pltpu.VMEM((8, BLK), F32),
            pltpu.VMEM((8, BLK), F32),
            pltpu.VMEM((REFB, D, BLK), BF16),
            pltpu.VMEM((8, BLK, D), BF16),
            pltpu.VMEM((RB, BLK, D), BF16),
            pltpu.VMEM((ENT, BLK, BLK), F32),
            [pltpu.VMEM((TOPC, BLK, BLK), F32)] * 4,
            [pltpu.VMEM((BLK, BLK), F32)] * 4,
            [pltpu.VMEM((BLK, BLK), F32)] * 4,
            pltpu.VMEM((REFB, BLK), F32),
            pltpu.VMEM((ENT, BLK), F32),
            pltpu.VMEM((ENT, BLK), F32),
            pltpu.VMEM((ENT, BLK), F32),
            pltpu.VMEM((ENT, BLK), F32),
            pltpu.VMEM((ENT, BLK), F32),
            pltpu.VMEM((BLK, ENT), BF16),
            pltpu.VMEM((RB, BLK, BLK), F32),
            pltpu.VMEM((RB, BLK, BLK), F32),
            pltpu.VMEM((RB, BLK, BLK), F32),
            pltpu.VMEM((RB, BLK, BLK), F32),
            pltpu.VMEM((3, REFB, BLK), F32),
            pltpu.VMEM((REFB, BLK), F32),
            pltpu.VMEM((3, NAR, 8, BLK), F32),
            pltpu.VMEM((3, 8, BLK), F32),
            pltpu.VMEM((3, GRP, 8, BLK), F32),
            pltpu.VMEM((2, 8, BLK), F32),
            pltpu.VMEM((2, REFB, BLK), F32),
            pltpu.SemaphoreType.REGULAR,
            dma((7,)),
            dma((1,)),
            dma((32,)),
            dma((30,)),
            dma((31,)),
            dma((31,)),
            dma((NAR,)),
            dma((NAR,)),
            dma((3, NAR)),
            dma((3, NAR)),
            dma((3, GRP)),
            dma((3, GRP)),
            dma((2, NAR)),
            dma((2, NAR)),
        ],
        compiler_params=pltpu.CompilerParams(
            collective_id=0, has_side_effects=True, vmem_limit_bytes=56 * 1024 * 1024
        ),
        name="sinkhorn",
    )(
        candidates.T,
        live_slots,
        run_desc.reshape(RB, BLK, D),
        ref_desc.reshape(8, BLK, D),
        run_mass.reshape(RB, BLK),
        ref_mass.reshape(8, BLK),
        ref_start.reshape(8, BLK),
    )
    run_potential, ref_potential = pl.pallas_call(
        write_out,
        out_shape=(
            jax.ShapeDtypeStruct((RB, BLK), F32),
            jax.ShapeDtypeStruct((8, BLK), F32),
        ),
        in_specs=[vmem, vmem],
        out_specs=(vmem, vmem),
        name="write_out",
    )(run_potential, ref_potential)
    return run_potential.reshape(-1), ref_potential.reshape(-1)


def solution(mesh):
    both = P(("grp", "nar"))
    wide = P(("grp", "nar"), None)
    return jax.shard_map(
        shards,
        mesh=mesh,
        in_specs=(wide, P("nar", None), wide, both, both, P("nar"), P("nar")),
        out_specs=(both, P("nar")),
        check_vma=False,
    )
```
